32 devices in a mesh: stn: 2 (over x), vox: 16 (over z, y, core).
Axes of the slice: x: 2, y: 2, z: 4, core: 2. Of those that a mesh axis runs over, the one named last changes fastest.
Arguments:
- voltages: bfloat16 [56, 2, 65536], P('stn', None, 'vox'), may hold values from -6 to 6
- sample_delays: int32 [56, 65536], P(None, 'vox'), may hold values from 0 to 239
- timing_offsets: int32 [56], replicated, may hold values from 0 to 15
- reference_station: int32 [1], replicated, may hold values from 0 to 55
Outputs:
- image_out: float32 [64, 65536], P('stn', 'vox')
The draws below stay inside these ranges and needn't reach their ends.
All inputs are finite; a program needn't handle non-finite values.
Results may differ from the reference program's by a relative error of at most 0.004.
Values may be sent and summed in bfloat16 or wider, within the bound.
No kernel may reach another device: no remote copies, remote signals or barrier semaphores. Data moves between devices by JAX's collectives and lax.ppermute only.
A program may use at most 64 MiB of HBM per device.

```python
import math
import jax
import jax.numpy as jnp
from jax import lax

STATIONS = 56
POLS = 2
WIN = 1024
LAGS = 256
OFFMAX = 16
NT = 65536
SLICES = 64
NV = 65536


def touch_ends(entries, stream_key, smallest, top_value):
    longest = entries.shape.index(max(entries.shape))
    spots = []
    for shift in (0, 1):
        where = [jax.random.randint(jax.random.fold_in(stream_key, axis), (), 0, length) for axis, length in enumerate(entries.shape)]
        where[longest] = (where[longest] + shift) % entries.shape[longest]
        spots.append(tuple(where))
    return entries.at[spots[0]].set(smallest).at[spots[1]].set(top_value)


def block_levels(rng, shape, pieces, least, largest):
    factor_of = 1.0
    for dim, shards_of in pieces:
        draws = jax.random.uniform(jax.random.fold_in(jax.random.fold_in(rng, 6), dim), (shards_of,), jnp.float32, least / len(pieces), largest / len(pieces))
        factor_of = factor_of * jnp.repeat(jnp.exp(draws), shape[dim] // shards_of).reshape((-1,) + (1,) * (len(shape) - 1 - dim))
    return factor_of


def bell_draw(rng, shape, scale, most, cuts=(), kind=jnp.bfloat16):
    factor_of = block_levels(rng, shape, cuts, -0.22, 0.18) if cuts else 1.0
    drawn = jax.random.normal(rng, shape, jnp.float32) * scale * factor_of
    return jnp.minimum(jnp.maximum(drawn, -most), most).astype(kind)


def setup_inputs(seed: int = 0) -> dict:
    key_of = jax.random.split(jax.random.key(seed), 5)
    voltages = bell_draw(key_of[0], (STATIONS, POLS, NT), 1.0, 6.0, ((0, 2), (2, 16)))
    sample_delays = touch_ends(jax.random.randint(key_of[1], (STATIONS, NV), 0, LAGS - OFFMAX), jax.random.fold_in(key_of[1], 1), 0, (LAGS - OFFMAX) - 1).astype(jnp.int32)
    timing_offsets = touch_ends(jax.random.randint(key_of[2], (STATIONS,), 0, OFFMAX), jax.random.fold_in(key_of[2], 1), 0, OFFMAX - 1).astype(jnp.int32)
    reference_station = jax.random.randint(key_of[3], (1,), 0, STATIONS).astype(jnp.int32)
    return dict(voltages=voltages, sample_delays=sample_delays, timing_offsets=timing_offsets, reference_station=reference_station)


def taper_weights(length):
    position = (jnp.arange(length, dtype=jnp.float32) + 0.5) / length
    return 0.5 - 0.5 * jnp.cos(2.0 * math.pi * position)

def reference(voltages, sample_delays, timing_offsets, reference_station):
    station_ref = reference_station[0]
    taper_curve = taper_weights(WIN)
    norm_inv = 1.0 / jnp.sqrt(jnp.sum(taper_curve * taper_curve))
    windowed = (voltages.reshape(STATIONS, POLS, SLICES, WIN).astype(jnp.float32) * taper_curve).astype(jnp.bfloat16)
    ref_signal = lax.dynamic_index_in_dim(voltages, station_ref, 0, keepdims=False)
    padded = jnp.pad(ref_signal, ((0, 0), (LAGS // 2, LAGS // 2 + WIN)))
    leading = padded[:, :NT].reshape(POLS, SLICES, WIN)
    trailing = padded[:, WIN:NT + WIN].reshape(POLS, SLICES, WIN)[:, :, :LAGS - 1]
    segments = jnp.concatenate([leading, trailing], axis=2).astype(jnp.float32)
    windowed_wide = windowed.astype(jnp.float32)

    def one_lag(lag_value):
        shifted = lax.dynamic_slice_in_dim(segments, lag_value, WIN, 2)
        return jnp.einsum('spkj,pkj->sk', windowed_wide, shifted)
    per_lag = lax.map(one_lag, jnp.arange(LAGS, dtype=jnp.int32))
    keep_mask = (jnp.arange(STATIONS, dtype=jnp.int32) != station_ref).astype(jnp.float32)
    correlations = (jnp.transpose(per_lag, (1, 2, 0)) * keep_mask[:, None, None] * norm_inv).astype(jnp.bfloat16)
    lag_index = sample_delays + timing_offsets[:, None]

    def add_station(station, running):
        corr_rows = lax.dynamic_index_in_dim(correlations, station, 0, keepdims=False).astype(jnp.float32)
        lag_picks = lax.dynamic_index_in_dim(lag_index, station, 0, keepdims=False)
        return running + jnp.take(corr_rows, lag_picks, axis=1)
    image_out = lax.fori_loop(0, STATIONS, add_station, jnp.zeros((SLICES, NV), jnp.float32))
    return image_out * (1.0 / math.sqrt(2.0 * STATIONS))
```

```python
import functools
import math

import jax
import jax.numpy as jnp
import numpy as np
from jax import lax
from jax.experimental import pallas as pl
from jax.experimental.pallas import tpu as pltpu
from jax.sharding import PartitionSpec as P

STATIONS = 56
WIN = 1024
LAGS = 256
HALF = LAGS // 2
LANES = 128
F8 = jnp.float8_e4m3fn
VMEM = pl.BlockSpec(memory_space=pltpu.VMEM)
SMEM = pl.BlockSpec(memory_space=pltpu.SMEM)


def taper_weights():
    position = (np.arange(WIN, dtype=np.float32) + np.float32(0.5)) / np.float32(WIN)
    return (0.5 - 0.5 * np.cos(2.0 * np.pi * position.astype(np.float64))).astype(np.float32)


def norm_inverse():
    taper = taper_weights()
    return float(np.float32(1.0) / np.sqrt(np.sum(taper * taper, dtype=np.float32)))


def lane_gather(table, index):
    return lax.gather(
        table,
        index[..., None],
        lax.GatherDimensionNumbers(
            offset_dims=(),
            collapsed_slice_dims=(1,),
            start_index_map=(1,),
            operand_batching_dims=(0,),
            start_indices_batching_dims=(0,),
        ),
        slice_sizes=(1, 1),
        mode=lax.GatherScatterMode.PROMISE_IN_BOUNDS,
    )


def corr_kernel(norm, ref_ref, win_ref, ext_ref, out_ref, rev_ref, shift_ref, rows_ref):
    pols, stations, samples = win_ref.shape
    slices = samples // WIN
    blocks = ext_ref.shape[1] // LANES
    pitch = rows_ref.shape[1] // slices
    mirror = LANES - 1 - lax.broadcasted_iota(jnp.int32, (8, LANES), 1)
    for m in range(blocks):
        piece = ext_ref[:, LANES * m : LANES * (m + 1)].astype(jnp.float32)
        piece = jnp.concatenate([piece] * (8 // pols), axis=0)
        at = LANES * (blocks - 1 - m)
        rev_ref[:, at : at + LANES] = lane_gather(piece, mirror)
    for p in range(pols):
        for m in range(blocks - 1):
            pair = jnp.broadcast_to(
                rev_ref[p : p + 1, LANES * m : LANES * (m + 2)], (LANES, 2 * LANES)
            )
            rolled = pltpu.roll(pair, 0, 1, stride=1, stride_axis=0)
            shift_ref[p, :, LANES * (m + 1) : LANES * (m + 2)] = rolled[:, LANES:].astype(
                jnp.bfloat16
            )
    station = lax.broadcasted_iota(jnp.int32, (stations, LAGS), 0)
    mine = ref_ref[0] - lax.axis_index("stn") * stations
    factor = jnp.where(station == mine, 0.0, norm)
    for k in range(slices):
        total = jnp.zeros((stations, LAGS), jnp.float32)
        for p in range(pols):
            for a in range(WIN // LAGS):
                first = WIN * k + LAGS * a
                at = samples - first
                hankel = jnp.concatenate(
                    [shift_ref[p, :, at : at + LAGS], shift_ref[p, :, at - LANES : at + LANES]],
                    axis=0,
                )
                total = total + jnp.dot(
                    win_ref[p, :, first : first + LAGS],
                    hankel,
                    preferred_element_type=jnp.float32,
                )
        total = total * factor
        for h in range(LAGS // LANES):
            rows_ref[h, pitch * k : pitch * k + stations, :] = total[
                :, LANES * h : LANES * (h + 1)
            ]
    for s in range(stations):
        for h in range(LAGS // LANES):
            at = LAGS * s + LANES * h
            out_ref[:, at : at + LANES] = rows_ref[h, pl.ds(s, slices, stride=pitch), :].astype(
                jnp.bfloat16
            )


def correlate(windowed, extended, reference_station):
    pols, stations, samples = windowed.shape
    slices = samples // WIN
    pitch = -(-stations // 8) * 8
    return pl.pallas_call(
        functools.partial(corr_kernel, norm_inverse()),
        out_shape=jax.ShapeDtypeStruct((slices, stations * LAGS), jnp.bfloat16),
        in_specs=[SMEM, VMEM, VMEM],
        out_specs=VMEM,
        scratch_shapes=[
            pltpu.VMEM((8, samples + LAGS), jnp.float32),
            pltpu.VMEM((pols, LANES, samples + LAGS), jnp.bfloat16),
            pltpu.VMEM((LAGS // LANES, pitch * slices, LANES), jnp.float32),
        ],
        cost_estimate=pl.CostEstimate(
            flops=2 * pols * stations * samples * LAGS,
            bytes_accessed=2 * pols * stations * samples,
            transcendentals=0,
        ),
        compiler_params=pltpu.CompilerParams(vmem_limit_bytes=24 << 20),
    )(reference_station, windowed, extended)


def image_kernel(
    swap, offset_ref, corr_ref, delay_ref, *refs
):
    *out_refs, rows_ref, pieces_ref, scale_ref, sums_ref = refs
    groups, slices_each, columns = corr_ref.shape
    total = groups * slices_each
    stations = columns // LAGS
    voxels = delay_ref.shape[1]
    stn = lax.axis_index("stn")
    half = total // 2
    first = stn * (half // slices_each) if swap else 0
    for j in range(groups):
        source = lax.rem(first + j, groups)
        rows_ref[slices_each * j : slices_each * (j + 1), :] = corr_ref[source].astype(jnp.float32)
    chunk = 32
    for r in range(0, total, chunk):
        block = rows_ref[r : r + chunk, :]
        top = jnp.maximum(jnp.max(jnp.abs(block), axis=1, keepdims=True), 1e-36)
        power = jnp.floor(jnp.log2(256.0 / top))
        up = jnp.exp2(power).astype(jnp.bfloat16).astype(jnp.float32)
        down = jnp.exp2(-power).astype(jnp.bfloat16).astype(jnp.float32)
        block = block * up
        coarse = block.astype(F8)
        pieces_ref[r : r + chunk, :] = coarse
        pieces_ref[total + r : total + r + chunk, :] = (
            (block - coarse.astype(jnp.float32)) * 16.0
        ).astype(F8)
        scale_ref[r : r + chunk, :] = jnp.broadcast_to(
            down * (1.0 / math.sqrt(2.0 * STATIONS)), (chunk, LANES)
        )
    level = (lax.broadcasted_iota(jnp.int32, (LAGS, voxels), 0) - HALF).astype(jnp.int8)
    one = jnp.ones((LAGS, voxels), F8)
    zero = jnp.zeros((LAGS, voxels), F8)
    sums = jnp.zeros((2 * total, voxels), jnp.float32)
    for s0 in range(0, stations, 2):
        hots = []
        for s in range(s0, min(s0 + 2, stations)):
            row = stn * stations + s
            where_to = (HALF - 1 - offset_ref[row]) - delay_ref[pl.ds(row, 1), :]
            where_to = jnp.broadcast_to(where_to, (32, voxels)).astype(jnp.int8)[0:1]
            hots.append(jnp.where(level == where_to, one, zero))
        hot = jnp.concatenate(hots, axis=0) if len(hots) > 1 else hots[0]
        sums = sums + jnp.dot(
            pieces_ref[:, LAGS * s0 : LAGS * s0 + hot.shape[0]],
            hot,
            preferred_element_type=jnp.float32,
        )
    sums_ref[...] = sums
    for r in range(0, total, 8):
        value = sums_ref[r : r + 8, :] + sums_ref[total + r : total + r + 8, :] * (1.0 / 16.0)
        value = value * scale_ref[r : r + 8, 0:1]
        if swap and r >= half:
            rows_ref_out = out_refs[1]
            if r % 16 == 0:
                upper = value
            else:
                rows_ref_out[r - half - 8 : r - half + 8, :] = jnp.concatenate(
                    [upper, value], axis=0
                ).astype(jnp.bfloat16)
        else:
            out_refs[0][r : r + 8, :] = value


def image(corr, sample_delays, timing_offsets, swap):
    groups, slices_each, columns = corr.shape
    total = groups * slices_each
    voxels = sample_delays.shape[1]
    if swap:
        out_shape = [
            jax.ShapeDtypeStruct((total // 2, voxels), jnp.float32),
            jax.ShapeDtypeStruct((total // 2, voxels), jnp.bfloat16),
        ]
    else:
        out_shape = [jax.ShapeDtypeStruct((total, voxels), jnp.float32)]
    return pl.pallas_call(
        functools.partial(image_kernel, swap),
        out_shape=out_shape,
        in_specs=[SMEM, VMEM, VMEM],
        out_specs=[VMEM] * len(out_shape),
        scratch_shapes=[
            pltpu.VMEM((total, columns), jnp.float32),
            pltpu.VMEM((2 * total, columns), F8),
            pltpu.VMEM((total, LANES), jnp.float32),
            pltpu.VMEM((2 * total, voxels), jnp.float32),
        ],
        cost_estimate=pl.CostEstimate(
            flops=4 * total * columns * voxels,
            bytes_accessed=4 * total * voxels,
            transcendentals=0,
        ),
        compiler_params=pltpu.CompilerParams(vmem_limit_bytes=56 << 20),
    )(timing_offsets, corr, sample_delays)


def neighbours(block, width):
    count = lax.axis_size("vox")
    forward = [(i, i + 1) for i in range(count - 1)]
    backward = [(target, source) for source, target in forward]
    low = lax.ppermute(block[:, block.shape[1] - width :], "vox", forward)
    high = lax.ppermute(block[:, :width], "vox", backward)
    return jnp.concatenate([low, block, high], axis=1)


def shards(voltages, sample_delays, timing_offsets, reference_station):
    stations_here, pols, samples_here = voltages.shape
    slices_here = samples_here // WIN
    stn_size = lax.axis_size("stn")
    station_ref = reference_station[0]
    owner = station_ref // stations_here
    swap = stn_size == 2

    candidate = lax.dynamic_index_in_dim(voltages, station_ref % stations_here, 0, keepdims=False)
    if swap:
        extended = neighbours(candidate, HALF)
        other = lax.ppermute(extended, "stn", [(0, 1), (1, 0)])
        extended = jnp.where(lax.axis_index("stn") == owner, extended, other)
    else:
        kept = jnp.where(lax.axis_index("stn") == owner, candidate, 0).astype(candidate.dtype)
        extended = neighbours(lax.psum(kept, "stn"), HALF)

    windowed = (
        voltages.reshape(stations_here, pols, slices_here, WIN).astype(jnp.float32)
        * taper_weights()
    ).astype(jnp.bfloat16)
    windowed = jnp.transpose(windowed.reshape(stations_here, pols, samples_here), (1, 0, 2))

    corr = correlate(windowed, extended, reference_station)
    gathered = lax.all_gather(corr, "vox", axis=0, tiled=False)
    if swap:
        kept, sent = image(gathered, sample_delays, timing_offsets, True)
        received = lax.ppermute(sent, "stn", [(0, 1), (1, 0)])
        return kept + received.astype(jnp.float32)
    (partial,) = image(gathered, sample_delays, timing_offsets, False)
    return lax.psum_scatter(partial, "stn", scatter_dimension=0, tiled=True)


def solution(mesh):
    return jax.shard_map(
        shards,
        mesh=mesh,
        in_specs=(P("stn", None, "vox"), P(None, "vox"), P(), P()),
        out_specs=P("stn", "vox"),
        check_vma=False,
    )
```

```python
import functools
import math

import jax
import jax.numpy as jnp
import numpy as np
from jax import lax
from jax.experimental import pallas as pl
from jax.experimental.pallas import tpu as pltpu
from jax.sharding import PartitionSpec as P

STATIONS = 56
WIN = 1024
LAGS = 256
HALF = LAGS // 2
LANES = 128
F8 = jnp.float8_e4m3fn
VMEM = pl.BlockSpec(memory_space=pltpu.VMEM)
SMEM = pl.BlockSpec(memory_space=pltpu.SMEM)


def taper_weights():
    position = (np.arange(WIN, dtype=np.float32) + np.float32(0.5)) / np.float32(WIN)
    return (0.5 - 0.5 * np.cos(2.0 * np.pi * position.astype(np.float64))).astype(np.float32)


def norm_inverse():
    taper = taper_weights()
    return float(np.float32(1.0) / np.sqrt(np.sum(taper * taper, dtype=np.float32)))


def lane_gather(table, index):
    return lax.gather(
        table,
        index[..., None],
        lax.GatherDimensionNumbers(
            offset_dims=(),
            collapsed_slice_dims=(1,),
            start_index_map=(1,),
            operand_batching_dims=(0,),
            start_indices_batching_dims=(0,),
        ),
        slice_sizes=(1, 1),
        mode=lax.GatherScatterMode.PROMISE_IN_BOUNDS,
    )


def corr_kernel(norm, ref_ref, win_ref, ext_ref, out_ref, rev_ref, shift_ref, rows_ref):
    pols, stations, samples = win_ref.shape
    slices = samples // WIN
    blocks = ext_ref.shape[1] // LANES
    pitch = rows_ref.shape[1] // slices
    mirror = LANES - 1 - lax.broadcasted_iota(jnp.int32, (8, LANES), 1)
    for m in range(blocks):
        piece = ext_ref[:, LANES * m : LANES * (m + 1)].astype(jnp.float32)
        piece = jnp.concatenate([piece] * (8 // pols), axis=0)
        at = LANES * (blocks - 1 - m)
        rev_ref[:, at : at + LANES] = lane_gather(piece, mirror)
    for p in range(pols):
        for m in range(blocks - 1):
            pair = jnp.broadcast_to(
                rev_ref[p : p + 1, LANES * m : LANES * (m + 2)], (LANES, 2 * LANES)
            )
            rolled = pltpu.roll(pair, 0, 1, stride=1, stride_axis=0)
            shift_ref[p, :, LANES * (m + 1) : LANES * (m + 2)] = rolled[:, LANES:].astype(
                jnp.bfloat16
            )
    station = lax.broadcasted_iota(jnp.int32, (stations, LAGS), 0)
    column = lax.broadcasted_iota(jnp.int32, (stations, LAGS), 1)
    mine = ref_ref[0] - lax.axis_index("stn") * stations
    factor = jnp.where((station == mine) | (column == 0), 0.0, norm)
    for k in range(slices):
        total = jnp.zeros((stations, LAGS), jnp.float32)
        for p in range(pols):
            for a in range(WIN // LAGS):
                first = WIN * k + LAGS * a
                at = samples - first
                hankel = jnp.concatenate(
                    [shift_ref[p, :, at : at + LAGS], shift_ref[p, :, at - LANES : at + LANES]],
                    axis=0,
                )
                total = total + jnp.dot(
                    win_ref[p, :, first : first + LAGS],
                    hankel,
                    preferred_element_type=jnp.float32,
                )
        total = total * factor
        top = jnp.max(jnp.max(jnp.abs(total), axis=1, keepdims=True), axis=0, keepdims=True)
        power = jnp.floor(jnp.log2(224.0 / jnp.maximum(top, 1e-35)))
        scale = jnp.exp2(power).astype(jnp.bfloat16).astype(jnp.float32)
        total = jnp.where(column == 0, power, total * scale)
        for h in range(LAGS // LANES):
            rows_ref[h, pitch * k : pitch * k + stations, :] = total[
                :, LANES * h : LANES * (h + 1)
            ]
    for s in range(stations):
        for h in range(LAGS // LANES):
            at = LAGS * s + LANES * h
            out_ref[:, at : at + LANES] = rows_ref[h, pl.ds(s, slices, stride=pitch), :].astype(
                jnp.bfloat16
            )


def correlate(windowed, extended, reference_station):
    pols, stations, samples = windowed.shape
    slices = samples // WIN
    pitch = -(-stations // 8) * 8
    return pl.pallas_call(
        functools.partial(corr_kernel, norm_inverse()),
        out_shape=jax.ShapeDtypeStruct((slices, stations * LAGS), jnp.bfloat16),
        in_specs=[SMEM, VMEM, VMEM],
        out_specs=VMEM,
        scratch_shapes=[
            pltpu.VMEM((8, samples + LAGS), jnp.float32),
            pltpu.VMEM((pols, LANES, samples + LAGS), jnp.bfloat16),
            pltpu.VMEM((LAGS // LANES, pitch * slices, LANES), jnp.float32),
        ],
        cost_estimate=pl.CostEstimate(
            flops=2 * pols * stations * samples * LAGS,
            bytes_accessed=2 * pols * stations * samples,
            transcendentals=0,
        ),
        compiler_params=pltpu.CompilerParams(vmem_limit_bytes=24 << 20),
    )(reference_station, windowed, extended)


def split_kernel(*refs):
    *block_refs, pieces_ref, scale_ref = refs
    stages = []
    for ref in block_refs:
        block = ref[...].astype(jnp.float32)
        coarse = block.astype(F8).astype(jnp.float32)
        stages.append(jnp.concatenate([coarse, (block - coarse) * 16.0], axis=0))
    pieces_ref[...] = jnp.concatenate(stages, axis=0).astype(F8)
    for d, ref in enumerate(block_refs):
        rows = ref.shape[0]
        power = ref[:, 0:LANES].astype(jnp.float32)[:, 0:1]
        down = jnp.exp2(-power).astype(jnp.bfloat16).astype(jnp.float32)
        down = jnp.broadcast_to(down * (1.0 / math.sqrt(2.0 * STATIONS)), (rows, LANES))
        scale_ref[2 * rows * d : 2 * rows * (d + 1), :] = jnp.concatenate(
            [down, down * (1.0 / 16.0)], axis=0
        )


def split(blocks):
    slices, columns = blocks[0].shape
    rows = 2 * slices * len(blocks)
    return pl.pallas_call(
        split_kernel,
        out_shape=[
            jax.ShapeDtypeStruct((rows, columns), F8),
            jax.ShapeDtypeStruct((rows, LANES), jnp.float32),
        ],
        in_specs=[VMEM] * len(blocks),
        out_specs=[VMEM] * 2,
        cost_estimate=pl.CostEstimate(
            flops=8 * rows * columns, bytes_accessed=2 * rows * columns, transcendentals=0
        ),
        compiler_params=pltpu.CompilerParams(vmem_limit_bytes=16 << 20),
    )(*blocks)


def target_kernel(offset_ref, delay_ref, out_ref):
    stations, rows, voxels = out_ref.shape
    for s in range(stations):
        row = lax.axis_index("stn") * stations + s
        target = (HALF - 1 - offset_ref[row]) - delay_ref[pl.ds(row, 1), :]
        out_ref[s] = jnp.broadcast_to(target, (rows, voxels)).astype(jnp.int8)


def targets(sample_delays, timing_offsets, stations):
    voxels = sample_delays.shape[1]
    return pl.pallas_call(
        target_kernel,
        out_shape=jax.ShapeDtypeStruct((stations, 32, voxels), jnp.int8),
        in_specs=[SMEM, VMEM],
        out_specs=VMEM,
        cost_estimate=pl.CostEstimate(
            flops=32 * stations * voxels, bytes_accessed=36 * stations * voxels, transcendentals=0
        ),
        compiler_params=pltpu.CompilerParams(vmem_limit_bytes=24 << 20),
    )(timing_offsets, sample_delays)


def image_kernel(swap, parts, target_ref, *refs):
    piece_refs, scale_refs = refs[:parts], refs[parts : 2 * parts]
    *out_refs, sums_ref = refs[2 * parts :]
    rows = piece_refs[0].shape[0]
    stations, tile, voxels = target_ref.shape
    level = (lax.broadcasted_iota(jnp.int32, (LAGS, voxels), 0) - HALF).astype(jnp.int8)
    one = jnp.ones((LAGS, voxels), F8)
    zero = jnp.zeros((LAGS, voxels), F8)
    sums = jnp.zeros((parts * rows, voxels), jnp.float32)
    for s0 in range(0, stations, 2):
        hots = []
        for s in range(s0, min(s0 + 2, stations)):
            target = jnp.concatenate([target_ref[s]] * (LAGS // tile), axis=0)
            hots.append(jnp.where(level == target, one, zero))
        hot = jnp.concatenate(hots, axis=0) if len(hots) > 1 else hots[0]
        at = LAGS * s0
        pieces = jnp.concatenate([ref[:, at : at + hot.shape[0]] for ref in piece_refs], axis=0)
        sums = sums + jnp.dot(pieces, hot, preferred_element_type=jnp.float32)
    for g in range(parts):
        for r in range(0, rows, 8):
            at = rows * g + r
            sums_ref[at : at + 8, :] = sums[at : at + 8, :] * scale_refs[g][r : r + 8, 0:1]
    mine = lax.axis_index("vox")
    groups = parts * rows // 8
    if swap:
        mine = mine ^ (lax.axis_index("stn") * (groups // 2))
    first = lax.broadcasted_iota(jnp.int32, (8, voxels), 0) < 4
    lower = None
    for j in range(0, groups, 2):
        here = sums_ref[pl.ds(pl.multiple_of(8 * (mine ^ j), 8), 8), :]
        there = sums_ref[pl.ds(pl.multiple_of(8 * (mine ^ (j + 1)), 8), 8), :]
        value = jnp.where(
            first,
            here + pltpu.roll(here, 4, 0),
            there + pltpu.roll(there, 4, 0),
        )
        if not swap or j < groups // 2:
            out_refs[0][4 * j : 4 * j + 8, :] = value
        elif lower is None:
            lower = value
        else:
            at = 4 * (j - groups // 2) - 8
            out_refs[1][at : at + 16, :] = jnp.concatenate([lower, value], axis=0).astype(
                jnp.bfloat16
            )
            lower = None


def image(pieces, scales, target, swap, part, count):
    rows, columns = pieces[0].shape
    total = len(pieces) * rows // 2
    stations, tile, voxels = target.shape
    voxels = voxels // count
    if swap:
        out_shape = [
            jax.ShapeDtypeStruct((total // 2, voxels), jnp.float32),
            jax.ShapeDtypeStruct((total // 2, voxels), jnp.bfloat16),
        ]
    else:
        out_shape = [jax.ShapeDtypeStruct((total, voxels), jnp.float32)]
    return pl.pallas_call(
        functools.partial(image_kernel, swap, len(pieces)),
        grid=(1,),
        out_shape=out_shape,
        in_specs=[pl.BlockSpec((stations, tile, voxels), lambda i: (0, 0, part))]
        + [VMEM] * (2 * len(pieces)),
        out_specs=[VMEM] * len(out_shape),
        scratch_shapes=[pltpu.VMEM((2 * total, voxels), jnp.float32)],
        cost_estimate=pl.CostEstimate(
            flops=4 * total * columns * voxels,
            bytes_accessed=4 * total * voxels,
            transcendentals=0,
        ),
        compiler_params=pltpu.CompilerParams(vmem_limit_bytes=48 << 20),
    )(target, *pieces, *scales)


def add_kernel(*refs):
    *in_refs, out_ref = refs
    at = 0
    for kept_ref, came_ref in zip(in_refs[::2], in_refs[1::2], strict=True):
        width = kept_ref.shape[1]
        out_ref[:, at : at + width] = kept_ref[...] + came_ref[...].astype(jnp.float32)
        at += width


def flip(block, axis, mask):
    count = lax.axis_size(axis)
    return lax.ppermute(block, axis, [(i, i ^ mask) for i in range(count)])


def extend_paired(candidate, owner):
    count = lax.axis_size("vox")
    odd = lax.axis_index("vox") % 2 == 1
    first, last = candidate[:, :HALF], candidate[:, candidate.shape[1] - HALF :]
    steps = [(b, b + 1) for b in range(1, count - 1, 2)] + [(b + 1, b) for b in range(1, count - 1, 2)]
    outer = jnp.where(odd, last, first)
    here = lax.ppermute(outer, "vox", steps)
    cross = [
        (x * count + source, (1 - x) * count + target) for x in range(2) for source, target in steps
    ]
    there = lax.ppermute(outer, ("stn", "vox"), cross)
    inner = flip(jnp.where(odd, first, last), "vox", 1)
    wide = jnp.concatenate([candidate, inner], axis=1)
    other = flip(wide, "stn", 1)
    mine = lax.axis_index("stn") == owner
    wide = jnp.where(mine, wide, other)
    outer = jnp.where(mine, here, there)
    body, inner = wide[:, : candidate.shape[1]], wide[:, candidate.shape[1] :]
    return jnp.concatenate(
        [jnp.where(odd, inner, outer), body, jnp.where(odd, outer, inner)], axis=1
    )


def extend(candidate, owner):
    kept = jnp.where(lax.axis_index("stn") == owner, candidate, 0).astype(candidate.dtype)
    block = lax.psum(kept, "stn")
    count = lax.axis_size("vox")
    forward = [(i, i + 1) for i in range(count - 1)]
    backward = [(target, source) for source, target in forward]
    low = lax.ppermute(block[:, block.shape[1] - HALF :], "vox", forward)
    high = lax.ppermute(block[:, :HALF], "vox", backward)
    return jnp.concatenate([low, block, high], axis=1)


def gather_paired(block):
    blocks = {0: block}
    for d in (12, 8, 4):
        blocks[d] = flip(block, "vox", d)
    for d in (0, 4, 8, 12):
        blocks[d | 2] = flip(blocks[d], "vox", 2)
    for d in (0, 2, 4, 6, 8, 10, 12, 14):
        blocks[d | 1] = flip(blocks[d], "vox", 1)
    return [[blocks[d] for d in order] for order in ORDER]


ORDER = ((0, 1, 2, 3), (4, 5, 6, 7), (8, 9, 10, 11), (12, 13, 14, 15))


def shards(voltages, sample_delays, timing_offsets, reference_station):
    stations_here, pols, samples_here = voltages.shape
    slices_here = samples_here // WIN
    count = lax.axis_size("vox")
    station_ref = reference_station[0]
    owner = station_ref // stations_here
    swap = lax.axis_size("stn") == 2 and count == 16

    candidate = lax.dynamic_index_in_dim(voltages, station_ref % stations_here, 0, keepdims=False)
    extended = extend_paired(candidate, owner) if swap else extend(candidate, owner)

    windowed = (
        voltages.reshape(stations_here, pols, slices_here, WIN).astype(jnp.float32)
        * taper_weights()
    ).astype(jnp.bfloat16)
    windowed = jnp.transpose(windowed.reshape(stations_here, pols, samples_here), (1, 0, 2))

    corr = correlate(windowed, extended, reference_station)
    target = targets(sample_delays, timing_offsets, stations_here)
    if swap:
        groups = gather_paired(corr)
    else:
        gathered = lax.all_gather(corr, "vox", axis=0, tiled=False)
        mine = lax.axis_index("vox")
        every = [
            lax.dynamic_index_in_dim(gathered, mine ^ j, 0, keepdims=False) for j in range(count)
        ]
        groups = [every[j : j + 4] for j in range(0, count, 4)]
    pieces, scales = zip(*[split(blocks) for blocks in groups], strict=True)
    if not swap:
        (partial,) = image(pieces, scales, target, False, 0, 1)
        return lax.psum_scatter(partial, "stn", scatter_dimension=0, tiled=True)
    operands = []
    for part in range(PARTS):
        kept, sent = image(pieces, scales, target, True, part, PARTS)
        operands += [kept, flip(sent, "stn", 1)]
    return pl.pallas_call(
        add_kernel,
        out_shape=jax.ShapeDtypeStruct((operands[0].shape[0], sample_delays.shape[1]), jnp.float32),
        in_specs=[VMEM] * len(operands),
        out_specs=VMEM,
        compiler_params=pltpu.CompilerParams(vmem_limit_bytes=16 << 20),
    )(*operands)


PARTS = 2


def solution(mesh):
    return jax.shard_map(
        shards,
        mesh=mesh,
        in_specs=(P("stn", None, "vox"), P(None, "vox"), P(), P()),
        out_specs=P("stn", "vox"),
        check_vma=False,
    )
```

```python
import functools
import math

import jax
import jax.numpy as jnp
import numpy as np
from jax import lax
from jax.experimental import pallas as pl
from jax.experimental.pallas import tpu as pltpu
from jax.sharding import PartitionSpec as P

STATIONS = 56
WIN = 1024
LAGS = 256
HALF = LAGS // 2
LANES = 128
F8 = jnp.float8_e4m3fn
VMEM = pl.BlockSpec(memory_space=pltpu.VMEM)
SMEM = pl.BlockSpec(memory_space=pltpu.SMEM)


def taper_weights():
    position = (np.arange(WIN, dtype=np.float32) + np.float32(0.5)) / np.float32(WIN)
    return (0.5 - 0.5 * np.cos(2.0 * np.pi * position.astype(np.float64))).astype(np.float32)


def norm_inverse():
    taper = taper_weights()
    return float(np.float32(1.0) / np.sqrt(np.sum(taper * taper, dtype=np.float32)))


def lane_gather(table, index):
    return lax.gather(
        table,
        index[..., None],
        lax.GatherDimensionNumbers(
            offset_dims=(),
            collapsed_slice_dims=(1,),
            start_index_map=(1,),
            operand_batching_dims=(0,),
            start_indices_batching_dims=(0,),
        ),
        slice_sizes=(1, 1),
        mode=lax.GatherScatterMode.PROMISE_IN_BOUNDS,
    )


def corr_kernel(norm, ref_ref, win_ref, ext_ref, out_ref, rev_ref, shift_ref, rows_ref):
    pols, stations, samples = win_ref.shape
    slices = samples // WIN
    blocks = ext_ref.shape[1] // LANES
    pitch = rows_ref.shape[1] // slices
    mirror = LANES - 1 - lax.broadcasted_iota(jnp.int32, (8, LANES), 1)
    for m in range(blocks):
        piece = ext_ref[:, LANES * m : LANES * (m + 1)].astype(jnp.float32)
        piece = jnp.concatenate([piece] * (8 // pols), axis=0)
        at = LANES * (blocks - 1 - m)
        rev_ref[:, at : at + LANES] = lane_gather(piece, mirror)
    for p in range(pols):
        for m in range(blocks - 1):
            pair = jnp.broadcast_to(
                rev_ref[p : p + 1, LANES * m : LANES * (m + 2)], (LANES, 2 * LANES)
            )
            rolled = pltpu.roll(pair, 0, 1, stride=1, stride_axis=0)
            shift_ref[p, :, LANES * (m + 1) : LANES * (m + 2)] = rolled[:, LANES:].astype(
                jnp.bfloat16
            )
    station = lax.broadcasted_iota(jnp.int32, (stations, LAGS), 0)
    column = lax.broadcasted_iota(jnp.int32, (stations, LAGS), 1)
    mine = ref_ref[0] - lax.axis_index("stn") * stations
    factor = jnp.where((station == mine) | (column == 0), 0.0, norm)
    for k in range(slices):
        total = jnp.zeros((stations, LAGS), jnp.float32)
        for p in range(pols):
            for a in range(WIN // LAGS):
                first = WIN * k + LAGS * a
                at = samples - first
                hankel = jnp.concatenate(
                    [shift_ref[p, :, at : at + LAGS], shift_ref[p, :, at - LANES : at + LANES]],
                    axis=0,
                )
                total = total + jnp.dot(
                    win_ref[p, :, first : first + LAGS],
                    hankel,
                    preferred_element_type=jnp.float32,
                )
        total = total * factor
        top = jnp.max(jnp.max(jnp.abs(total), axis=1, keepdims=True), axis=0, keepdims=True)
        power = jnp.floor(jnp.log2(224.0 / jnp.maximum(top, 1e-35)))
        scale = jnp.exp2(power).astype(jnp.bfloat16).astype(jnp.float32)
        total = jnp.where(column == 0, power, total * scale)
        for h in range(LAGS // LANES):
            rows_ref[h, pitch * k : pitch * k + stations, :] = total[
                :, LANES * h : LANES * (h + 1)
            ]
    for s in range(stations):
        for h in range(LAGS // LANES):
            at = LAGS * s + LANES * h
            out_ref[:, at : at + LANES] = rows_ref[h, pl.ds(s, slices, stride=pitch), :].astype(
                jnp.bfloat16
            )


def correlate(windowed, extended, reference_station):
    pols, stations, samples = windowed.shape
    slices = samples // WIN
    pitch = -(-stations // 8) * 8
    return pl.pallas_call(
        functools.partial(corr_kernel, norm_inverse()),
        out_shape=jax.ShapeDtypeStruct((slices, stations * LAGS), jnp.bfloat16),
        in_specs=[SMEM, VMEM, VMEM],
        out_specs=VMEM,
        scratch_shapes=[
            pltpu.VMEM((8, samples + LAGS), jnp.float32),
            pltpu.VMEM((pols, LANES, samples + LAGS), jnp.bfloat16),
            pltpu.VMEM((LAGS // LANES, pitch * slices, LANES), jnp.float32),
        ],
        cost_estimate=pl.CostEstimate(
            flops=2 * pols * stations * samples * LAGS,
            bytes_accessed=2 * pols * stations * samples,
            transcendentals=0,
        ),
        compiler_params=pltpu.CompilerParams(vmem_limit_bytes=24 << 20),
    )(reference_station, windowed, extended)


def split_kernel(*refs):
    *block_refs, pieces_ref, scale_ref = refs
    stages = []
    for ref in block_refs:
        block = ref[...].astype(jnp.float32)
        coarse = block.astype(F8).astype(jnp.float32)
        stages.append(jnp.concatenate([coarse, (block - coarse) * 16.0], axis=0))
    pieces_ref[...] = jnp.concatenate(stages, axis=0).astype(F8)
    for d, ref in enumerate(block_refs):
        rows = ref.shape[0]
        power = ref[:, 0:LANES].astype(jnp.float32)[:, 0:1]
        down = jnp.exp2(-power).astype(jnp.bfloat16).astype(jnp.float32)
        down = jnp.broadcast_to(down * (1.0 / math.sqrt(2.0 * STATIONS)), (rows, LANES))
        scale_ref[2 * rows * d : 2 * rows * (d + 1), :] = jnp.concatenate(
            [down, down * (1.0 / 16.0)], axis=0
        )


def split(blocks):
    slices, columns = blocks[0].shape
    rows = 2 * slices * len(blocks)
    return pl.pallas_call(
        split_kernel,
        out_shape=[
            jax.ShapeDtypeStruct((rows, columns), F8),
            jax.ShapeDtypeStruct((rows, LANES), jnp.float32),
        ],
        in_specs=[VMEM] * len(blocks),
        out_specs=[VMEM] * 2,
        cost_estimate=pl.CostEstimate(
            flops=8 * rows * columns, bytes_accessed=2 * rows * columns, transcendentals=0
        ),
        compiler_params=pltpu.CompilerParams(vmem_limit_bytes=16 << 20),
    )(*blocks)


def target_kernel(offset_ref, delay_ref, out_ref):
    stations, rows, voxels = out_ref.shape
    for s in range(stations):
        row = lax.axis_index("stn") * stations + s
        target = (HALF - 1 - offset_ref[row]) - delay_ref[pl.ds(row, 1), :]
        out_ref[s] = jnp.broadcast_to(target, (rows, voxels)).astype(jnp.int8)


def targets(sample_delays, timing_offsets, stations):
    voxels = sample_delays.shape[1]
    return pl.pallas_call(
        target_kernel,
        out_shape=jax.ShapeDtypeStruct((stations, 32, voxels), jnp.int8),
        in_specs=[SMEM, VMEM],
        out_specs=VMEM,
        cost_estimate=pl.CostEstimate(
            flops=32 * stations * voxels, bytes_accessed=36 * stations * voxels, transcendentals=0
        ),
        compiler_params=pltpu.CompilerParams(vmem_limit_bytes=24 << 20),
    )(timing_offsets, sample_delays)


def image_kernel(swap, parts, start, target_ref, *refs):
    piece_refs, scale_refs = refs[:parts], refs[parts : 2 * parts]
    *out_refs, sums_ref = refs[2 * parts :]
    rows = piece_refs[0].shape[0]
    stations, tile, _ = target_ref.shape
    voxels = sums_ref.shape[1]
    level = (lax.broadcasted_iota(jnp.int32, (LAGS, voxels), 0) - HALF).astype(jnp.int8)
    one = jnp.ones((LAGS, voxels), F8)
    zero = jnp.zeros((LAGS, voxels), F8)
    sums = jnp.zeros((parts * rows, voxels), jnp.float32)
    for s0 in range(0, stations, 2):
        hots = []
        for s in range(s0, min(s0 + 2, stations)):
            target = jnp.concatenate([target_ref[s, :, start : start + voxels]] * (LAGS // tile), axis=0)
            hots.append(jnp.where(level == target, one, zero))
        hot = jnp.concatenate(hots, axis=0) if len(hots) > 1 else hots[0]
        at = LAGS * s0
        pieces = jnp.concatenate([ref[:, at : at + hot.shape[0]] for ref in piece_refs], axis=0)
        sums = sums + jnp.dot(pieces, hot, preferred_element_type=jnp.float32)
    for g in range(parts):
        for r in range(0, rows, 8):
            at = rows * g + r
            sums_ref[at : at + 8, :] = sums[at : at + 8, :] * scale_refs[g][r : r + 8, 0:1]
    mine = lax.axis_index("vox")
    groups = parts * rows // 8
    if swap:
        mine = mine ^ (lax.axis_index("stn") * (groups // 2))
    first = lax.broadcasted_iota(jnp.int32, (8, voxels), 0) < 4
    lower = None
    for j in range(0, groups, 2):
        here, there = mine ^ j, mine ^ (j + 1)
        if swap:
            here, there = [(d & 3) * 4 + d // 4 for d in (here, there)]
        here = sums_ref[pl.ds(pl.multiple_of(8 * here, 8), 8), :]
        there = sums_ref[pl.ds(pl.multiple_of(8 * there, 8), 8), :]
        value = jnp.where(
            first,
            here + pltpu.roll(here, 4, 0),
            there + pltpu.roll(there, 4, 0),
        )
        if not swap or j < groups // 2:
            out_refs[0][4 * j : 4 * j + 8, :] = value
        elif lower is None:
            lower = value
        else:
            at = 4 * (j - groups // 2) - 8
            out_refs[1][at : at + 16, :] = jnp.concatenate([lower, value], axis=0).astype(
                jnp.bfloat16
            )
            lower = None


def image(pieces, scales, target, swap, start, voxels):
    rows, columns = pieces[0].shape
    total = len(pieces) * rows // 2
    if swap:
        out_shape = [
            jax.ShapeDtypeStruct((total // 2, voxels), jnp.float32),
            jax.ShapeDtypeStruct((total // 2, voxels), jnp.bfloat16),
        ]
    else:
        out_shape = [jax.ShapeDtypeStruct((total, voxels), jnp.float32)]
    return pl.pallas_call(
        functools.partial(image_kernel, swap, len(pieces), start),
        out_shape=out_shape,
        in_specs=[VMEM] * (1 + 2 * len(pieces)),
        out_specs=[VMEM] * len(out_shape),
        scratch_shapes=[pltpu.VMEM((2 * total, voxels), jnp.float32)],
        cost_estimate=pl.CostEstimate(
            flops=4 * total * columns * voxels,
            bytes_accessed=4 * total * voxels,
            transcendentals=0,
        ),
        compiler_params=pltpu.CompilerParams(vmem_limit_bytes=48 << 20),
    )(target, *pieces, *scales)


def add_kernel(*refs):
    *in_refs, out_ref = refs
    at = 0
    for kept_ref, came_ref in zip(in_refs[::2], in_refs[1::2], strict=True):
        width = kept_ref.shape[1]
        out_ref[:, at : at + width] = kept_ref[...] + came_ref[...].astype(jnp.float32)
        at += width


def flip(block, axis, mask):
    count = lax.axis_size(axis)
    return lax.ppermute(block, axis, [(i, i ^ mask) for i in range(count)])


def extend_paired(candidate, owner):
    count = lax.axis_size("vox")
    odd = lax.axis_index("vox") % 2 == 1
    first, last = candidate[:, :HALF], candidate[:, candidate.shape[1] - HALF :]
    steps = [(b, b + 1) for b in range(1, count - 1, 2)] + [(b + 1, b) for b in range(1, count - 1, 2)]
    outer = lax.ppermute(jnp.where(odd, last, first), "vox", steps)
    inner = flip(jnp.where(odd, first, last), "vox", 1)
    low, high = jnp.where(odd, inner, outer), jnp.where(odd, outer, inner)
    extended = jnp.concatenate([low, candidate, high], axis=1)
    other = flip(extended, "stn", 1)
    return jnp.where(lax.axis_index("stn") == owner, extended, other)


def extend(candidate, owner):
    kept = jnp.where(lax.axis_index("stn") == owner, candidate, 0).astype(candidate.dtype)
    block = lax.psum(kept, "stn")
    count = lax.axis_size("vox")
    forward = [(i, i + 1) for i in range(count - 1)]
    backward = [(target, source) for source, target in forward]
    low = lax.ppermute(block[:, block.shape[1] - HALF :], "vox", forward)
    high = lax.ppermute(block[:, :HALF], "vox", backward)
    return jnp.concatenate([low, block, high], axis=1)


def gather_paired(block):
    blocks = {0: block}
    for d in (12, 8, 4):
        blocks[d] = flip(block, "vox", d)
    for d in (0, 4, 8, 12):
        blocks[d | 2] = flip(blocks[d], "vox", 2)
    for d in (0, 4, 8, 12, 2, 6):
        blocks[d | 1] = flip(blocks[d], "vox", 1)
    done = [split([blocks[d] for d in order]) for order in ORDER[:2]]
    blocks[10], blocks[14], done = lax.optimization_barrier((blocks[10], blocks[14], done))
    for d in (10, 14):
        blocks[d | 1] = flip(blocks[d], "vox", 1)
    return done + [split([blocks[d] for d in order]) for order in ORDER[2:]]


ORDER = ((0, 4, 8, 12), (1, 5, 9, 13), (2, 6, 10, 14), (3, 7, 11, 15))


def shards(voltages, sample_delays, timing_offsets, reference_station):
    stations_here, pols, samples_here = voltages.shape
    slices_here = samples_here // WIN
    count = lax.axis_size("vox")
    station_ref = reference_station[0]
    owner = station_ref // stations_here
    swap = lax.axis_size("stn") == 2 and count == 16

    candidate = lax.dynamic_index_in_dim(voltages, station_ref % stations_here, 0, keepdims=False)
    extended = extend_paired(candidate, owner) if swap else extend(candidate, owner)

    windowed = (
        voltages.reshape(stations_here, pols, slices_here, WIN).astype(jnp.float32)
        * taper_weights()
    ).astype(jnp.bfloat16)
    windowed = jnp.transpose(windowed.reshape(stations_here, pols, samples_here), (1, 0, 2))

    target = targets(sample_delays, timing_offsets, stations_here)
    extended, target = lax.optimization_barrier((extended, target))
    corr = correlate(windowed, extended, reference_station)
    if swap:
        pairs = gather_paired(corr)
    else:
        gathered = lax.all_gather(corr, "vox", axis=0, tiled=False)
        mine = lax.axis_index("vox")
        every = [
            lax.dynamic_index_in_dim(gathered, mine ^ j, 0, keepdims=False) for j in range(count)
        ]
        pairs = [split(every[j : j + 4]) for j in range(0, count, 4)]
    pieces, scales = zip(*pairs, strict=True)
    if not swap:
        (partial,) = image(pieces, scales, target, False, 0, sample_delays.shape[1])
        return lax.psum_scatter(partial, "stn", scatter_dimension=0, tiled=True)
    operands = []
    start = 0
    for share in SHARES:
        voxels = sample_delays.shape[1] * share // sum(SHARES)
        kept, sent = image(pieces, scales, target, True, start, voxels)
        operands += [kept, flip(sent, "stn", 1)]
        start += voxels
    return pl.pallas_call(
        add_kernel,
        out_shape=jax.ShapeDtypeStruct((operands[0].shape[0], sample_delays.shape[1]), jnp.float32),
        in_specs=[VMEM] * len(operands),
        out_specs=VMEM,
        compiler_params=pltpu.CompilerParams(vmem_limit_bytes=16 << 20),
    )(*operands)


SHARES = (9, 7)


def solution(mesh):
    return jax.shard_map(
        shards,
        mesh=mesh,
        in_specs=(P("stn", None, "vox"), P(None, "vox"), P(), P()),
        out_specs=P("stn", "vox"),
        check_vma=False,
    )
```

```python
import functools
import math

import jax
import jax.numpy as jnp
import numpy as np
from jax import lax
from jax.experimental import pallas as pl
from jax.experimental.pallas import tpu as pltpu
from jax.sharding import PartitionSpec as P

STATIONS = 56
WIN = 1024
LAGS = 256
HALF = LAGS // 2
LANES = 128
F8 = jnp.float8_e4m3fn
VMEM = pl.BlockSpec(memory_space=pltpu.VMEM)
SMEM = pl.BlockSpec(memory_space=pltpu.SMEM)


def taper_weights():
    position = (np.arange(WIN, dtype=np.float32) + np.float32(0.5)) / np.float32(WIN)
    return (0.5 - 0.5 * np.cos(2.0 * np.pi * position.astype(np.float64))).astype(np.float32)


def norm_inverse():
    taper = taper_weights()
    return float(np.float32(1.0) / np.sqrt(np.sum(taper * taper, dtype=np.float32)))


def lane_gather(table, index):
    return lax.gather(
        table,
        index[..., None],
        lax.GatherDimensionNumbers(
            offset_dims=(),
            collapsed_slice_dims=(1,),
            start_index_map=(1,),
            operand_batching_dims=(0,),
            start_indices_batching_dims=(0,),
        ),
        slice_sizes=(1, 1),
        mode=lax.GatherScatterMode.PROMISE_IN_BOUNDS,
    )


def reverse_block(block):
    mirror = LANES - 1 - lax.broadcasted_iota(jnp.int32, (8, LANES), 1)
    piece = block.astype(jnp.float32)
    return lane_gather(jnp.concatenate([piece] * (8 // piece.shape[0]), axis=0), mirror)


def shifted_copies(pair):
    pair = jnp.broadcast_to(pair, (LANES, 2 * LANES))
    return pltpu.roll(pair, 0, 1, stride=1, stride_axis=0)[:, LANES:].astype(jnp.bfloat16)


def chunk_product(windowed, left, middle, right):
    hankel = jnp.concatenate(
        [jnp.concatenate([middle, right], axis=1), jnp.concatenate([left, middle], axis=1)], axis=0
    )
    return jnp.dot(windowed, hankel, preferred_element_type=jnp.float32)


def corr_kernel(win_ref, ref_ref, out_ref, rev_ref, shift_ref):
    pols, stations, samples = win_ref.shape
    slices = samples // WIN
    pitch = out_ref.shape[0] // slices
    blocks = samples // LANES
    for m in range(blocks):
        at = LANES * (blocks - 1 - m)
        rev_ref[:, at : at + LANES] = reverse_block(ref_ref[:, LANES * m : LANES * (m + 1)])
    for p in range(pols):
        for m in range(1, blocks):
            shift_ref[p, :, LANES * m : LANES * (m + 1)] = shifted_copies(
                rev_ref[p : p + 1, LANES * (m - 1) : LANES * (m + 1)]
            )
    chunks = WIN // LAGS
    for k in range(slices):
        total = jnp.zeros((stations, LAGS), jnp.float32)
        for p in range(pols):
            for a in range(chunks):
                if (k, a) in ((0, 0), (slices - 1, chunks - 1)):
                    continue
                first = WIN * k + LAGS * a
                at = samples - first - LANES
                total = total + chunk_product(
                    win_ref[p, :, first : first + LAGS],
                    shift_ref[p, :, at - LANES : at],
                    shift_ref[p, :, at : at + LANES],
                    shift_ref[p, :, at + LANES : at + 2 * LANES],
                )
        out_ref[pitch * k : pitch * k + stations, :] = total


def finish_kernel(norm, ref_ref, win_ref, body_ref, low_ref, high_ref, part_ref, out_ref, rows_ref):
    pols, stations, samples = win_ref.shape
    slices = samples // WIN
    pitch = part_ref.shape[0] // slices
    early = [reverse_block(body_ref[:, LANES * m : LANES * (m + 1)]) for m in (2, 1, 0)]
    early.append(reverse_block(low_ref[...]))
    ends = samples - LANES
    late = [reverse_block(high_ref[...])]
    late += [
        reverse_block(body_ref[:, ends - LANES * m : ends - LANES * (m - 1)]) for m in (0, 1, 2)
    ]
    extra = []
    for first, row in ((0, early), (samples - LAGS, late)):
        total = jnp.zeros((stations, LAGS), jnp.float32)
        for p in range(pols):
            copies = [
                shifted_copies(jnp.concatenate([row[m][p : p + 1], row[m + 1][p : p + 1]], axis=1))
                for m in range(3)
            ]
            total = total + chunk_product(win_ref[p, :, first : first + LAGS], *copies)
        extra.append(total)
    station = lax.broadcasted_iota(jnp.int32, (stations, LAGS), 0)
    column = lax.broadcasted_iota(jnp.int32, (stations, LAGS), 1)
    mine = ref_ref[0] - lax.axis_index("stn") * stations
    factor = jnp.where((station == mine) | (column == 0), 0.0, norm)
    for k in range(slices):
        total = part_ref[pitch * k : pitch * k + stations, :]
        if k == 0:
            total = total + extra[0]
        if k == slices - 1:
            total = total + extra[1]
        total = total * factor
        top = jnp.max(jnp.max(jnp.abs(total), axis=1, keepdims=True), axis=0, keepdims=True)
        power = jnp.floor(jnp.log2(224.0 / jnp.maximum(top, 1e-35)))
        scale = jnp.exp2(power).astype(jnp.bfloat16).astype(jnp.float32)
        total = jnp.where(column == 0, power, total * scale)
        for h in range(LAGS // LANES):
            rows_ref[h, pitch * k : pitch * k + stations, :] = total[
                :, LANES * h : LANES * (h + 1)
            ]
    for s in range(stations):
        for h in range(LAGS // LANES):
            at = LAGS * s + LANES * h
            out_ref[:, at : at + LANES] = rows_ref[h, pl.ds(s, slices, stride=pitch), :].astype(
                jnp.bfloat16
            )


def correlate(windowed, body, halos, reference_station):
    pols, stations, samples = windowed.shape
    slices = samples // WIN
    pitch = -(-stations // 8) * 8
    params = pltpu.CompilerParams(vmem_limit_bytes=24 << 20)
    part = pl.pallas_call(
        corr_kernel,
        out_shape=jax.ShapeDtypeStruct((pitch * slices, LAGS), jnp.float32),
        in_specs=[VMEM, VMEM],
        out_specs=VMEM,
        scratch_shapes=[
            pltpu.VMEM((8, samples), jnp.float32),
            pltpu.VMEM((pols, LANES, samples), jnp.bfloat16),
        ],
        cost_estimate=pl.CostEstimate(
            flops=2 * pols * stations * samples * LAGS,
            bytes_accessed=2 * pols * stations * samples,
            transcendentals=0,
        ),
        compiler_params=params,
    )(windowed, body)
    return pl.pallas_call(
        functools.partial(finish_kernel, norm_inverse()),
        out_shape=jax.ShapeDtypeStruct((slices, stations * LAGS), jnp.bfloat16),
        in_specs=[SMEM] + [VMEM] * 5,
        out_specs=VMEM,
        scratch_shapes=[pltpu.VMEM((LAGS // LANES, pitch * slices, LANES), jnp.float32)],
        cost_estimate=pl.CostEstimate(
            flops=4 * pols * stations * LAGS * LAGS,
            bytes_accessed=2 * pols * stations * LAGS,
            transcendentals=0,
        ),
        compiler_params=params,
    )(reference_station, windowed, body, *halos, part)


def split_kernel(*refs):
    *block_refs, pieces_ref, scale_ref = refs
    stages = []
    for ref in block_refs:
        block = ref[...].astype(jnp.float32)
        coarse = block.astype(F8).astype(jnp.float32)
        stages.append(jnp.concatenate([coarse, (block - coarse) * 16.0], axis=0))
    pieces_ref[...] = jnp.concatenate(stages, axis=0).astype(F8)
    for d, ref in enumerate(block_refs):
        rows = ref.shape[0]
        power = ref[:, 0:LANES].astype(jnp.float32)[:, 0:1]
        down = jnp.exp2(-power).astype(jnp.bfloat16).astype(jnp.float32)
        down = jnp.broadcast_to(down * (1.0 / math.sqrt(2.0 * STATIONS)), (rows, LANES))
        scale_ref[2 * rows * d : 2 * rows * (d + 1), :] = jnp.concatenate(
            [down, down * (1.0 / 16.0)], axis=0
        )


def split(blocks):
    slices, columns = blocks[0].shape
    rows = 2 * slices * len(blocks)
    return pl.pallas_call(
        split_kernel,
        out_shape=[
            jax.ShapeDtypeStruct((rows, columns), F8),
            jax.ShapeDtypeStruct((rows, LANES), jnp.float32),
        ],
        in_specs=[VMEM] * len(blocks),
        out_specs=[VMEM] * 2,
        cost_estimate=pl.CostEstimate(
            flops=8 * rows * columns, bytes_accessed=2 * rows * columns, transcendentals=0
        ),
        compiler_params=pltpu.CompilerParams(vmem_limit_bytes=16 << 20),
    )(*blocks)


def target_kernel(stations, offset_ref, delay_ref, out_ref, rows_ref, offsets_ref, semaphores):
    rows = rows_ref.shape[0]
    tile, voxels = out_ref.shape[1:]
    first = lax.axis_index("stn") * stations
    start = pl.multiple_of(jnp.minimum(first // 8, (delay_ref.shape[0] - rows) // 8) * 8, 8)
    copies = [
        pltpu.make_async_copy(delay_ref.at[pl.ds(start, rows), :], rows_ref, semaphores.at[0]),
        pltpu.make_async_copy(offset_ref, offsets_ref, semaphores.at[1]),
    ]
    for copy in copies:
        copy.start()
    for copy in copies:
        copy.wait()
    for s in range(stations):
        delays = rows_ref[pl.ds(first - start + s, 1), :]
        target = (HALF - 1 - offsets_ref[first + s]) - delays
        out_ref[s] = jnp.broadcast_to(target, (tile, voxels)).astype(jnp.int8)


def targets(sample_delays, timing_offsets, stations):
    total, voxels = sample_delays.shape
    slack = max(a * stations % 8 for a in range(total // stations))
    rows = min(-(-(slack + stations) // 8) * 8, total)
    return pl.pallas_call(
        functools.partial(target_kernel, stations),
        out_shape=jax.ShapeDtypeStruct((stations, 32, voxels), jnp.int8),
        in_specs=[pl.BlockSpec(memory_space=pltpu.HBM)] * 2,
        out_specs=VMEM,
        scratch_shapes=[
            pltpu.VMEM((rows, voxels), jnp.int32),
            pltpu.SMEM(timing_offsets.shape, jnp.int32),
            pltpu.SemaphoreType.DMA((2,)),
        ],
        cost_estimate=pl.CostEstimate(
            flops=32 * stations * voxels, bytes_accessed=36 * stations * voxels, transcendentals=0
        ),
        compiler_params=pltpu.CompilerParams(vmem_limit_bytes=24 << 20),
    )(timing_offsets, sample_delays)


def image_kernel(swap, parts, start, target_ref, *refs):
    piece_refs, scale_refs = refs[:parts], refs[parts : 2 * parts]
    *out_refs, sums_ref = refs[2 * parts :]
    rows = piece_refs[0].shape[0]
    stations, tile, _ = target_ref.shape
    voxels = sums_ref.shape[1]
    level = (lax.broadcasted_iota(jnp.int32, (LAGS, voxels), 0) - HALF).astype(jnp.int8)
    one = jnp.ones((LAGS, voxels), F8)
    zero = jnp.zeros((LAGS, voxels), F8)
    sums = jnp.zeros((parts * rows, voxels), jnp.float32)
    for s0 in range(0, stations, 2):
        hots = []
        for s in range(s0, min(s0 + 2, stations)):
            target = jnp.concatenate([target_ref[s, :, start : start + voxels]] * (LAGS // tile), axis=0)
            hots.append(jnp.where(level == target, one, zero))
        hot = jnp.concatenate(hots, axis=0) if len(hots) > 1 else hots[0]
        at = LAGS * s0
        pieces = jnp.concatenate([ref[:, at : at + hot.shape[0]] for ref in piece_refs], axis=0)
        sums = sums + jnp.dot(pieces, hot, preferred_element_type=jnp.float32)
    for g in range(parts):
        for r in range(0, rows, 8):
            at = rows * g + r
            sums_ref[at : at + 8, :] = sums[at : at + 8, :] * scale_refs[g][r : r + 8, 0:1]
    mine = lax.axis_index("vox")
    groups = parts * rows // 8
    if swap:
        mine = mine ^ (lax.axis_index("stn") * (groups // 2))
    first = lax.broadcasted_iota(jnp.int32, (8, voxels), 0) < 4
    lower = None
    for j in range(0, groups, 2):
        here, there = mine ^ j, mine ^ (j + 1)
        if swap:
            here, there = [(d & 3) * 4 + d // 4 for d in (here, there)]
        here = sums_ref[pl.ds(pl.multiple_of(8 * here, 8), 8), :]
        there = sums_ref[pl.ds(pl.multiple_of(8 * there, 8), 8), :]
        value = jnp.where(
            first,
            here + pltpu.roll(here, 4, 0),
            there + pltpu.roll(there, 4, 0),
        )
        if not swap or j < groups // 2:
            out_refs[0][4 * j : 4 * j + 8, :] = value
        elif lower is None:
            lower = value
        else:
            at = 4 * (j - groups // 2) - 8
            out_refs[1][at : at + 16, :] = jnp.concatenate([lower, value], axis=0).astype(
                jnp.bfloat16
            )
            lower = None


def image(pieces, scales, target, swap, start, voxels):
    rows, columns = pieces[0].shape
    total = len(pieces) * rows // 2
    if swap:
        out_shape = [
            jax.ShapeDtypeStruct((total // 2, voxels), jnp.float32),
            jax.ShapeDtypeStruct((total // 2, voxels), jnp.bfloat16),
        ]
    else:
        out_shape = [jax.ShapeDtypeStruct((total, voxels), jnp.float32)]
    return pl.pallas_call(
        functools.partial(image_kernel, swap, len(pieces), start),
        out_shape=out_shape,
        in_specs=[VMEM] * (1 + 2 * len(pieces)),
        out_specs=[VMEM] * len(out_shape),
        scratch_shapes=[pltpu.VMEM((2 * total, voxels), jnp.float32)],
        cost_estimate=pl.CostEstimate(
            flops=4 * total * columns * voxels,
            bytes_accessed=4 * total * voxels,
            transcendentals=0,
        ),
        compiler_params=pltpu.CompilerParams(vmem_limit_bytes=48 << 20),
    )(target, *pieces, *scales)


def add_kernel(*refs):
    *in_refs, out_ref = refs
    at = 0
    for kept_ref, came_ref in zip(in_refs[::2], in_refs[1::2], strict=True):
        width = kept_ref.shape[1]
        out_ref[:, at : at + width] = kept_ref[...] + came_ref[...].astype(jnp.float32)
        at += width


def flip(block, axis, mask):
    count = lax.axis_size(axis)
    return lax.ppermute(block, axis, [(i, i ^ mask) for i in range(count)])


def halos_paired(body):
    count = lax.axis_size("vox")
    odd = lax.axis_index("vox") % 2 == 1
    first, last = body[:, :HALF], body[:, body.shape[1] - HALF :]
    steps = [(b, b + 1) for b in range(1, count - 1, 2)]
    steps += [(target, source) for source, target in steps]
    outer = lax.ppermute(jnp.where(odd, last, first), "vox", steps)
    inner = flip(jnp.where(odd, first, last), "vox", 1)
    return jnp.where(odd, inner, outer), jnp.where(odd, outer, inner)


def after(value, *others):
    return lax.optimization_barrier((value, *others))[0]


def gather_paired(block, sample_delays, timing_offsets, stations):
    blocks = {0: block}
    for d in (12, 8, 4, 2):
        blocks[d] = flip(block, "vox", d)
    blocks[1] = flip(block, "vox", 1)
    blocks[6] = flip(blocks[4], "vox", 2)
    target = targets(after(sample_delays, blocks[4]), timing_offsets, stations)
    near, target = lax.optimization_barrier((blocks[8], blocks[4], target, blocks[1]))[::2]
    blocks[10] = flip(near, "vox", 2)
    far = after(blocks[12], near)
    blocks[14] = flip(far, "vox", 2)
    blocks[2], blocks[4], blocks[6], blocks[8], blocks[12] = lax.optimization_barrier(
        (blocks[2], blocks[4], blocks[6], near, far)
    )
    for d in (2, 4, 6):
        blocks[d | 1] = flip(blocks[d], "vox", 1)
    early = split([blocks[d] for d in ORDER[0]])
    blocks[8], blocks[10], early, blocks[12] = lax.optimization_barrier(
        (blocks[8], blocks[10], early, blocks[12])
    )
    for d in (8, 10, 12):
        blocks[d | 1] = flip(blocks[d], "vox", 1)
    middle = split([blocks[d] for d in ORDER[1]])
    blocks[14], blocks[13] = lax.optimization_barrier((blocks[14], blocks[13]))
    blocks[15] = flip(blocks[14], "vox", 1)
    return [early, middle] + [split([blocks[d] for d in order]) for order in ORDER[2:]], target


ORDER = ((0, 4, 8, 12), (1, 5, 9, 13), (2, 6, 10, 14), (3, 7, 11, 15))


def shards(voltages, sample_delays, timing_offsets, reference_station):
    stations_here, pols, samples_here = voltages.shape
    slices_here = samples_here // WIN
    count = lax.axis_size("vox")
    station_ref = reference_station[0]
    owner = station_ref // stations_here
    swap = lax.axis_size("stn") == 2 and count == 16

    candidate = lax.dynamic_index_in_dim(voltages, station_ref % stations_here, 0, keepdims=False)
    candidate = lax.optimization_barrier(candidate)
    mine = lax.axis_index("stn") == owner
    if swap:
        body = jnp.where(mine, candidate, flip(candidate, "stn", 1))
        halos = halos_paired(body)
    else:
        body = lax.psum(jnp.where(mine, candidate, 0).astype(candidate.dtype), "stn")
        forward = [(i, i + 1) for i in range(count - 1)]
        backward = [(target, source) for source, target in forward]
        halos = (
            lax.ppermute(body[:, samples_here - HALF :], "vox", forward),
            lax.ppermute(body[:, :HALF], "vox", backward),
        )

    taper = np.tile(taper_weights(), slices_here)
    windowed = (voltages.astype(jnp.float32) * taper).astype(jnp.bfloat16)
    windowed = jnp.transpose(windowed, (1, 0, 2))

    corr = correlate(windowed, body, halos, reference_station)
    if swap:
        pairs, target = gather_paired(corr, sample_delays, timing_offsets, stations_here)
    else:
        target = targets(sample_delays, timing_offsets, stations_here)
        gathered = lax.all_gather(corr, "vox", axis=0, tiled=False)
        place = lax.axis_index("vox")
        every = [
            lax.dynamic_index_in_dim(gathered, place ^ j, 0, keepdims=False) for j in range(count)
        ]
        pairs = [split(every[j : j + 4]) for j in range(0, count, 4)]
    pieces, scales = zip(*pairs, strict=True)
    if not swap:
        (partial,) = image(pieces, scales, target, False, 0, sample_delays.shape[1])
        return lax.psum_scatter(partial, "stn", scatter_dimension=0, tiled=True)
    operands = []
    start = 0
    for share in SHARES:
        voxels = sample_delays.shape[1] * share // sum(SHARES)
        kept, sent = image(pieces, scales, target, True, start, voxels)
        operands += [kept, flip(sent, "stn", 1)]
        start += voxels
    return pl.pallas_call(
        add_kernel,
        out_shape=jax.ShapeDtypeStruct((operands[0].shape[0], sample_delays.shape[1]), jnp.float32),
        in_specs=[VMEM] * len(operands),
        out_specs=VMEM,
        compiler_params=pltpu.CompilerParams(vmem_limit_bytes=16 << 20),
    )(*operands)


SHARES = (9, 7)


def solution(mesh):
    return jax.shard_map(
        shards,
        mesh=mesh,
        in_specs=(P("stn", None, "vox"), P(None, "vox"), P(), P()),
        out_specs=P("stn", "vox"),
        check_vma=False,
    )
```

```python
import functools
import math

import jax
import jax.numpy as jnp
import numpy as np
from jax import lax
from jax.experimental import pallas as pl
from jax.experimental.pallas import tpu as pltpu
from jax.sharding import PartitionSpec as P

STATIONS = 56
WIN = 1024
LAGS = 256
HALF = LAGS // 2
LANES = 128
F8 = jnp.float8_e4m3fn
VMEM = pl.BlockSpec(memory_space=pltpu.VMEM)
SMEM = pl.BlockSpec(memory_space=pltpu.SMEM)


def taper_weights():
    position = (np.arange(WIN, dtype=np.float32) + np.float32(0.5)) / np.float32(WIN)
    return (0.5 - 0.5 * np.cos(2.0 * np.pi * position.astype(np.float64))).astype(np.float32)


def norm_inverse():
    taper = taper_weights()
    return float(np.float32(1.0) / np.sqrt(np.sum(taper * taper, dtype=np.float32)))


def lane_gather(table, index):
    return lax.gather(
        table,
        index[..., None],
        lax.GatherDimensionNumbers(
            offset_dims=(),
            collapsed_slice_dims=(1,),
            start_index_map=(1,),
            operand_batching_dims=(0,),
            start_indices_batching_dims=(0,),
        ),
        slice_sizes=(1, 1),
        mode=lax.GatherScatterMode.PROMISE_IN_BOUNDS,
    )


def reverse_block(block):
    mirror = LANES - 1 - lax.broadcasted_iota(jnp.int32, (8, LANES), 1)
    piece = block.astype(jnp.float32)
    return lane_gather(jnp.concatenate([piece] * (8 // piece.shape[0]), axis=0), mirror)


def shifted_copies(pair):
    pair = jnp.broadcast_to(pair, (LANES, 2 * LANES))
    return pltpu.roll(pair, 0, 1, stride=1, stride_axis=0)[:, LANES:].astype(jnp.bfloat16)


def chunk_product(windowed, left, middle, right):
    hankel = jnp.concatenate(
        [jnp.concatenate([middle, right], axis=1), jnp.concatenate([left, middle], axis=1)], axis=0
    )
    return jnp.dot(windowed, hankel, preferred_element_type=jnp.float32)


def corr_kernel(win_ref, ref_ref, out_ref, rev_ref, shift_ref):
    pols, stations, samples = win_ref.shape
    slices = samples // WIN
    pitch = out_ref.shape[0] // slices
    blocks = samples // LANES
    for m in range(blocks):
        at = LANES * (blocks - 1 - m)
        rev_ref[:, at : at + LANES] = reverse_block(ref_ref[:, LANES * m : LANES * (m + 1)])
    for p in range(pols):
        for m in range(1, blocks):
            shift_ref[p, :, LANES * m : LANES * (m + 1)] = shifted_copies(
                rev_ref[p : p + 1, LANES * (m - 1) : LANES * (m + 1)]
            )
    chunks = WIN // LAGS
    for k in range(slices):
        total = jnp.zeros((stations, LAGS), jnp.float32)
        for p in range(pols):
            for a in range(chunks):
                if (k, a) in ((0, 0), (slices - 1, chunks - 1)):
                    continue
                first = WIN * k + LAGS * a
                at = samples - first - LANES
                total = total + chunk_product(
                    win_ref[p, :, first : first + LAGS],
                    shift_ref[p, :, at - LANES : at],
                    shift_ref[p, :, at : at + LANES],
                    shift_ref[p, :, at + LANES : at + 2 * LANES],
                )
        out_ref[pitch * k : pitch * k + stations, :] = total


def finish_kernel(norm, ref_ref, win_ref, body_ref, low_ref, high_ref, part_ref, out_ref, rows_ref):
    pols, stations, samples = win_ref.shape
    slices = samples // WIN
    pitch = part_ref.shape[0] // slices
    early = [reverse_block(body_ref[:, LANES * m : LANES * (m + 1)]) for m in (2, 1, 0)]
    early.append(reverse_block(low_ref[...]))
    ends = samples - LANES
    late = [reverse_block(high_ref[...])]
    late += [
        reverse_block(body_ref[:, ends - LANES * m : ends - LANES * (m - 1)]) for m in (0, 1, 2)
    ]
    extra = []
    for first, row in ((0, early), (samples - LAGS, late)):
        total = jnp.zeros((stations, LAGS), jnp.float32)
        for p in range(pols):
            copies = [
                shifted_copies(jnp.concatenate([row[m][p : p + 1], row[m + 1][p : p + 1]], axis=1))
                for m in range(3)
            ]
            total = total + chunk_product(win_ref[p, :, first : first + LAGS], *copies)
        extra.append(total)
    station = lax.broadcasted_iota(jnp.int32, (stations, LAGS), 0)
    column = lax.broadcasted_iota(jnp.int32, (stations, LAGS), 1)
    mine = ref_ref[0] - lax.axis_index("stn") * stations
    factor = jnp.where((station == mine) | (column == 0), 0.0, norm)
    for k in range(slices):
        total = part_ref[pitch * k : pitch * k + stations, :]
        if k == 0:
            total = total + extra[0]
        if k == slices - 1:
            total = total + extra[1]
        total = total * factor
        top = jnp.max(jnp.max(jnp.abs(total), axis=1, keepdims=True), axis=0, keepdims=True)
        power = jnp.floor(jnp.log2(224.0 / jnp.maximum(top, 1e-35)))
        scale = jnp.exp2(power).astype(jnp.bfloat16).astype(jnp.float32)
        total = jnp.where(column == 0, power, total * scale)
        for h in range(LAGS // LANES):
            rows_ref[h, pitch * k : pitch * k + stations, :] = total[
                :, LANES * h : LANES * (h + 1)
            ]
    for s in range(stations):
        for h in range(LAGS // LANES):
            at = LAGS * s + LANES * h
            out_ref[:, at : at + LANES] = rows_ref[h, pl.ds(s, slices, stride=pitch), :].astype(
                jnp.bfloat16
            )


def correlate(windowed, body, halos, reference_station):
    pols, stations, samples = windowed.shape
    slices = samples // WIN
    pitch = -(-stations // 8) * 8
    params = pltpu.CompilerParams(vmem_limit_bytes=24 << 20)
    part = pl.pallas_call(
        corr_kernel,
        out_shape=jax.ShapeDtypeStruct((pitch * slices, LAGS), jnp.float32),
        in_specs=[VMEM, VMEM],
        out_specs=VMEM,
        scratch_shapes=[
            pltpu.VMEM((8, samples), jnp.float32),
            pltpu.VMEM((pols, LANES, samples), jnp.bfloat16),
        ],
        cost_estimate=pl.CostEstimate(
            flops=2 * pols * stations * samples * LAGS,
            bytes_accessed=2 * pols * stations * samples,
            transcendentals=0,
        ),
        compiler_params=params,
    )(windowed, body)
    return pl.pallas_call(
        functools.partial(finish_kernel, norm_inverse()),
        out_shape=jax.ShapeDtypeStruct((slices, stations * LAGS), jnp.bfloat16),
        in_specs=[SMEM] + [VMEM] * 5,
        out_specs=VMEM,
        scratch_shapes=[pltpu.VMEM((LAGS // LANES, pitch * slices, LANES), jnp.float32)],
        cost_estimate=pl.CostEstimate(
            flops=4 * pols * stations * LAGS * LAGS,
            bytes_accessed=2 * pols * stations * LAGS,
            transcendentals=0,
        ),
        compiler_params=params,
    )(reference_station, windowed, body, *halos, part)


def split_kernel(*refs):
    *block_refs, pieces_ref, scale_ref = refs
    stages = []
    for ref in block_refs:
        block = ref[...].astype(jnp.float32)
        coarse = block.astype(F8).astype(jnp.float32)
        stages.append(jnp.concatenate([coarse, (block - coarse) * 16.0], axis=0))
    pieces_ref[...] = jnp.concatenate(stages, axis=0).astype(F8)
    for d, ref in enumerate(block_refs):
        rows = ref.shape[0]
        power = ref[:, 0:LANES].astype(jnp.float32)[:, 0:1]
        down = jnp.exp2(-power).astype(jnp.bfloat16).astype(jnp.float32)
        down = jnp.broadcast_to(down * (1.0 / math.sqrt(2.0 * STATIONS)), (rows, LANES))
        scale_ref[2 * rows * d : 2 * rows * (d + 1), :] = jnp.concatenate(
            [down, down * (1.0 / 16.0)], axis=0
        )


def split(blocks):
    slices, columns = blocks[0].shape
    rows = 2 * slices * len(blocks)
    return pl.pallas_call(
        split_kernel,
        out_shape=[
            jax.ShapeDtypeStruct((rows, columns), F8),
            jax.ShapeDtypeStruct((rows, LANES), jnp.float32),
        ],
        in_specs=[VMEM] * len(blocks),
        out_specs=[VMEM] * 2,
        cost_estimate=pl.CostEstimate(
            flops=8 * rows * columns, bytes_accessed=2 * rows * columns, transcendentals=0
        ),
        compiler_params=pltpu.CompilerParams(vmem_limit_bytes=16 << 20),
    )(*blocks)


def target_kernel(stations, offset_ref, delay_ref, out_ref, rows_ref, offsets_ref, semaphores):
    rows = rows_ref.shape[0]
    tile, voxels = out_ref.shape[1:]
    first = lax.axis_index("stn") * stations
    start = pl.multiple_of(jnp.minimum(first // 8, (delay_ref.shape[0] - rows) // 8) * 8, 8)
    copies = [
        pltpu.make_async_copy(delay_ref.at[pl.ds(start, rows), :], rows_ref, semaphores.at[0]),
        pltpu.make_async_copy(offset_ref, offsets_ref, semaphores.at[1]),
    ]
    for copy in copies:
        copy.start()
    for copy in copies:
        copy.wait()
    for s in range(stations):
        delays = rows_ref[pl.ds(first - start + s, 1), :]
        target = (HALF - 1 - offsets_ref[first + s]) - delays
        out_ref[s] = jnp.broadcast_to(target, (tile, voxels)).astype(jnp.int8)


def targets(sample_delays, timing_offsets, stations):
    total, voxels = sample_delays.shape
    slack = max(a * stations % 8 for a in range(total // stations))
    rows = min(-(-(slack + stations) // 8) * 8, total)
    return pl.pallas_call(
        functools.partial(target_kernel, stations),
        out_shape=jax.ShapeDtypeStruct((stations, 32, voxels), jnp.int8),
        in_specs=[pl.BlockSpec(memory_space=pltpu.HBM)] * 2,
        out_specs=VMEM,
        scratch_shapes=[
            pltpu.VMEM((rows, voxels), jnp.int32),
            pltpu.SMEM(timing_offsets.shape, jnp.int32),
            pltpu.SemaphoreType.DMA((2,)),
        ],
        cost_estimate=pl.CostEstimate(
            flops=32 * stations * voxels, bytes_accessed=36 * stations * voxels, transcendentals=0
        ),
        compiler_params=pltpu.CompilerParams(vmem_limit_bytes=24 << 20),
    )(timing_offsets, sample_delays)


def image_kernel(swap, parts, start, target_ref, *refs):
    piece_refs, scale_refs = refs[:parts], refs[parts : 2 * parts]
    *out_refs, sums_ref = refs[2 * parts :]
    rows = piece_refs[0].shape[0]
    stations, tile, _ = target_ref.shape
    voxels = sums_ref.shape[1]
    level = (lax.broadcasted_iota(jnp.int32, (LAGS, voxels), 0) - HALF).astype(jnp.int8)
    one = jnp.ones((LAGS, voxels), F8)
    zero = jnp.zeros((LAGS, voxels), F8)
    sums = jnp.zeros((parts * rows, voxels), jnp.float32)
    for s0 in range(0, stations, 2):
        hots = []
        for s in range(s0, min(s0 + 2, stations)):
            target = jnp.concatenate([target_ref[s, :, start : start + voxels]] * (LAGS // tile), axis=0)
            hots.append(jnp.where(level == target, one, zero))
        hot = jnp.concatenate(hots, axis=0) if len(hots) > 1 else hots[0]
        at = LAGS * s0
        pieces = jnp.concatenate([ref[:, at : at + hot.shape[0]] for ref in piece_refs], axis=0)
        sums = sums + jnp.dot(pieces, hot, preferred_element_type=jnp.float32)
    for g in range(parts):
        for r in range(0, rows, 8):
            at = rows * g + r
            sums_ref[at : at + 8, :] = sums[at : at + 8, :] * scale_refs[g][r : r + 8, 0:1]
    mine = lax.axis_index("vox")
    groups = parts * rows // 8
    if swap:
        mine = mine ^ (lax.axis_index("stn") * (groups // 2))
    first = lax.broadcasted_iota(jnp.int32, (8, voxels), 0) < 4
    lower = None
    for j in range(0, groups, 2):
        here, there = mine ^ j, mine ^ (j + 1)
        if swap:
            here, there = [(d & 3) * 4 + d // 4 for d in (here, there)]
        here = sums_ref[pl.ds(pl.multiple_of(8 * here, 8), 8), :]
        there = sums_ref[pl.ds(pl.multiple_of(8 * there, 8), 8), :]
        value = jnp.where(
            first,
            here + pltpu.roll(here, 4, 0),
            there + pltpu.roll(there, 4, 0),
        )
        if not swap or j < groups // 2:
            out_refs[0][4 * j : 4 * j + 8, :] = value
        elif lower is None:
            lower = value
        else:
            at = 4 * (j - groups // 2) - 8
            out_refs[1][at : at + 16, :] = jnp.concatenate([lower, value], axis=0).astype(
                jnp.bfloat16
            )
            lower = None


def image(pieces, scales, target, swap, start, voxels):
    rows, columns = pieces[0].shape
    total = len(pieces) * rows // 2
    if swap:
        out_shape = [
            jax.ShapeDtypeStruct((total // 2, voxels), jnp.float32),
            jax.ShapeDtypeStruct((total // 2, voxels), jnp.bfloat16),
        ]
    else:
        out_shape = [jax.ShapeDtypeStruct((total, voxels), jnp.float32)]
    return pl.pallas_call(
        functools.partial(image_kernel, swap, len(pieces), start),
        out_shape=out_shape,
        in_specs=[VMEM] * (1 + 2 * len(pieces)),
        out_specs=[VMEM] * len(out_shape),
        scratch_shapes=[pltpu.VMEM((2 * total, voxels), jnp.float32)],
        cost_estimate=pl.CostEstimate(
            flops=4 * total * voxels,
            bytes_accessed=total,
            transcendentals=0,
        ),
        compiler_params=pltpu.CompilerParams(vmem_limit_bytes=48 << 20),
    )(target, *pieces, *scales)


def add_kernel(start, kept_ref, came_ref, *refs):
    out_ref, total_ref, semaphore = refs[-3:]
    total_ref[...] = kept_ref[...] + came_ref[...].astype(jnp.float32)
    copy = pltpu.make_async_copy(
        total_ref, out_ref.at[:, pl.ds(start, total_ref.shape[1])], semaphore
    )
    copy.start()
    copy.wait()


def add_part(kept, came, out, start, voxels):
    anywhere = pl.BlockSpec(memory_space=pltpu.HBM)
    before = () if out is None else (out,)
    return pl.pallas_call(
        functools.partial(add_kernel, start),
        out_shape=jax.ShapeDtypeStruct((kept.shape[0], voxels), jnp.float32),
        in_specs=[VMEM, VMEM] + [anywhere] * len(before),
        out_specs=anywhere,
        scratch_shapes=[pltpu.VMEM(kept.shape, jnp.float32), pltpu.SemaphoreType.DMA],
        input_output_aliases={2: 0} if before else {},
        cost_estimate=pl.CostEstimate(
            flops=kept.size, bytes_accessed=4 * kept.size, transcendentals=0
        ),
        compiler_params=pltpu.CompilerParams(vmem_limit_bytes=16 << 20),
    )(kept, came, *before)


def flip(block, axis, mask):
    count = lax.axis_size(axis)
    return lax.ppermute(block, axis, [(i, i ^ mask) for i in range(count)])


def halos_paired(body):
    count = lax.axis_size("vox")
    odd = lax.axis_index("vox") % 2 == 1
    first, last = body[:, :HALF], body[:, body.shape[1] - HALF :]
    steps = [(b, b + 1) for b in range(1, count - 1, 2)]
    steps += [(target, source) for source, target in steps]
    outer = lax.ppermute(jnp.where(odd, last, first), "vox", steps)
    inner = flip(jnp.where(odd, first, last), "vox", 1)
    return jnp.where(odd, inner, outer), jnp.where(odd, outer, inner)


def after(value, *others):
    return lax.optimization_barrier((value, *others))[0]


def gather_paired(block, sample_delays, timing_offsets, stations):
    blocks = {0: block}
    for d in (12, 8, 4, 2):
        blocks[d] = flip(block, "vox", d)
    blocks[1] = flip(block, "vox", 1)
    blocks[6] = flip(blocks[4], "vox", 2)
    target = targets(after(sample_delays, blocks[4]), timing_offsets, stations)
    near, target = lax.optimization_barrier((blocks[8], blocks[4], target, blocks[1]))[::2]
    blocks[10] = flip(near, "vox", 2)
    far = after(blocks[12], near)
    blocks[14] = flip(far, "vox", 2)
    blocks[2], blocks[4], blocks[6], blocks[8], blocks[12] = lax.optimization_barrier(
        (blocks[2], blocks[4], blocks[6], near, far)
    )
    for d in (2, 4, 6):
        blocks[d | 1] = flip(blocks[d], "vox", 1)
    early = split([blocks[d] for d in ORDER[0]])
    gate = lax.optimization_barrier((blocks[8], blocks[12], early, blocks[5]))
    blocks[8], blocks[12], early = gate[:3]
    for d in (8, 12):
        blocks[d | 1] = flip(blocks[d], "vox", 1)
    blocks[11] = flip(blocks[10], "vox", 1)
    blocks[14] = after(blocks[14], blocks[11], blocks[13])
    blocks[15] = flip(blocks[14], "vox", 1)
    middle = split([blocks[d] for d in ORDER[1]])
    return [early, middle] + [split([blocks[d] for d in order]) for order in ORDER[2:]], target


ORDER = ((0, 4, 8, 12), (1, 5, 9, 13), (2, 6, 10, 14), (3, 7, 11, 15))


def shards(voltages, sample_delays, timing_offsets, reference_station):
    stations_here, pols, samples_here = voltages.shape
    slices_here = samples_here // WIN
    count = lax.axis_size("vox")
    station_ref = reference_station[0]
    owner = station_ref // stations_here
    swap = lax.axis_size("stn") == 2 and count == 16

    candidate = lax.dynamic_index_in_dim(voltages, station_ref % stations_here, 0, keepdims=False)
    candidate = lax.optimization_barrier(candidate)
    mine = lax.axis_index("stn") == owner
    if swap:
        body = jnp.where(mine, candidate, flip(candidate, "stn", 1))
        halos = halos_paired(body)
    else:
        body = lax.psum(jnp.where(mine, candidate, 0).astype(candidate.dtype), "stn")
        forward = [(i, i + 1) for i in range(count - 1)]
        backward = [(target, source) for source, target in forward]
        halos = (
            lax.ppermute(body[:, samples_here - HALF :], "vox", forward),
            lax.ppermute(body[:, :HALF], "vox", backward),
        )

    taper = np.tile(taper_weights(), slices_here)
    windowed = (voltages.astype(jnp.float32) * taper).astype(jnp.bfloat16)
    windowed = jnp.transpose(windowed, (1, 0, 2))

    corr = correlate(windowed, body, halos, reference_station)
    if swap:
        pairs, target = gather_paired(corr, sample_delays, timing_offsets, stations_here)
    else:
        target = targets(sample_delays, timing_offsets, stations_here)
        gathered = lax.all_gather(corr, "vox", axis=0, tiled=False)
        place = lax.axis_index("vox")
        every = [
            lax.dynamic_index_in_dim(gathered, place ^ j, 0, keepdims=False) for j in range(count)
        ]
        pairs = [split(every[j : j + 4]) for j in range(0, count, 4)]
    pieces, scales = zip(*pairs, strict=True)
    if not swap:
        (partial,) = image(pieces, scales, target, False, 0, sample_delays.shape[1])
        return lax.psum_scatter(partial, "stn", scatter_dimension=0, tiled=True)
    parts = []
    start = 0
    for share in SHARES:
        voxels = sample_delays.shape[1] * share // sum(SHARES)
        kept, sent = image(pieces, scales, target, True, start, voxels)
        parts.append((start, kept, flip(sent, "stn", 1)))
        start += voxels
    out = None
    for start, kept, came in parts:
        out = add_part(kept, came, out, start, sample_delays.shape[1])
    return out


SHARES = (14, 10, 8)


def solution(mesh):
    return jax.shard_map(
        shards,
        mesh=mesh,
        in_specs=(P("stn", None, "vox"), P(None, "vox"), P(), P()),
        out_specs=P("stn", "vox"),
        check_vma=False,
    )
```

```python
import functools
import math

import jax
import jax.numpy as jnp
import numpy as np
from jax import lax
from jax.experimental import pallas as pl
from jax.experimental.pallas import tpu as pltpu
from jax.sharding import PartitionSpec as P

STATIONS = 56
WIN = 1024
LAGS = 256
HALF = LAGS // 2
LANES = 128
F8 = jnp.float8_e4m3fn
VMEM = pl.BlockSpec(memory_space=pltpu.VMEM)
SMEM = pl.BlockSpec(memory_space=pltpu.SMEM)


def taper_weights():
    position = (np.arange(WIN, dtype=np.float32) + np.float32(0.5)) / np.float32(WIN)
    return (0.5 - 0.5 * np.cos(2.0 * np.pi * position.astype(np.float64))).astype(np.float32)


def norm_inverse():
    taper = taper_weights()
    return float(np.float32(1.0) / np.sqrt(np.sum(taper * taper, dtype=np.float32)))


def lane_gather(table, index):
    return lax.gather(
        table,
        index[..., None],
        lax.GatherDimensionNumbers(
            offset_dims=(),
            collapsed_slice_dims=(1,),
            start_index_map=(1,),
            operand_batching_dims=(0,),
            start_indices_batching_dims=(0,),
        ),
        slice_sizes=(1, 1),
        mode=lax.GatherScatterMode.PROMISE_IN_BOUNDS,
    )


def reverse_block(block):
    mirror = LANES - 1 - lax.broadcasted_iota(jnp.int32, (8, LANES), 1)
    piece = block.astype(jnp.float32)
    return lane_gather(jnp.concatenate([piece] * (8 // piece.shape[0]), axis=0), mirror)


def shifted_copies(pair):
    pair = jnp.broadcast_to(pair, (LANES, 2 * LANES))
    return pltpu.roll(pair, 0, 1, stride=1, stride_axis=0)[:, LANES:].astype(jnp.bfloat16)


def chunk_product(windowed, left, middle, right):
    hankel = jnp.concatenate(
        [jnp.concatenate([middle, right], axis=1), jnp.concatenate([left, middle], axis=1)], axis=0
    )
    return jnp.dot(windowed, hankel, preferred_element_type=jnp.float32)


def corr_kernel(win_ref, ref_ref, out_ref, rev_ref, shift_ref):
    pols, stations, samples = win_ref.shape
    slices = samples // WIN
    pitch = out_ref.shape[0] // slices
    blocks = samples // LANES
    for m in range(blocks):
        at = LANES * (blocks - 1 - m)
        rev_ref[:, at : at + LANES] = reverse_block(ref_ref[:, LANES * m : LANES * (m + 1)])
    for p in range(pols):
        for m in range(1, blocks):
            shift_ref[p, :, LANES * m : LANES * (m + 1)] = shifted_copies(
                rev_ref[p : p + 1, LANES * (m - 1) : LANES * (m + 1)]
            )
    chunks = WIN // LAGS
    for k in range(slices):
        total = jnp.zeros((stations, LAGS), jnp.float32)
        for p in range(pols):
            for a in range(chunks):
                if (k, a) in ((0, 0), (slices - 1, chunks - 1)):
                    continue
                first = WIN * k + LAGS * a
                at = samples - first - LANES
                total = total + chunk_product(
                    win_ref[p, :, first : first + LAGS],
                    shift_ref[p, :, at - LANES : at],
                    shift_ref[p, :, at : at + LANES],
                    shift_ref[p, :, at + LANES : at + 2 * LANES],
                )
        out_ref[pitch * k : pitch * k + stations, :] = total


def finish_kernel(norm, ref_ref, win_ref, body_ref, low_ref, high_ref, part_ref, out_ref, rows_ref):
    pols, stations, samples = win_ref.shape
    slices = samples // WIN
    pitch = part_ref.shape[0] // slices
    early = [reverse_block(body_ref[:, LANES * m : LANES * (m + 1)]) for m in (2, 1, 0)]
    early.append(reverse_block(low_ref[...]))
    ends = samples - LANES
    late = [reverse_block(high_ref[...])]
    late += [
        reverse_block(body_ref[:, ends - LANES * m : ends - LANES * (m - 1)]) for m in (0, 1, 2)
    ]
    extra = []
    for first, row in ((0, early), (samples - LAGS, late)):
        total = jnp.zeros((stations, LAGS), jnp.float32)
        for p in range(pols):
            copies = [
                shifted_copies(jnp.concatenate([row[m][p : p + 1], row[m + 1][p : p + 1]], axis=1))
                for m in range(3)
            ]
            total = total + chunk_product(win_ref[p, :, first : first + LAGS], *copies)
        extra.append(total)
    station = lax.broadcasted_iota(jnp.int32, (stations, LAGS), 0)
    column = lax.broadcasted_iota(jnp.int32, (stations, LAGS), 1)
    mine = ref_ref[0] - lax.axis_index("stn") * stations
    factor = jnp.where((station == mine) | (column == 0), 0.0, norm)
    for k in range(slices):
        total = part_ref[pitch * k : pitch * k + stations, :]
        if k == 0:
            total = total + extra[0]
        if k == slices - 1:
            total = total + extra[1]
        total = total * factor
        top = jnp.max(jnp.max(jnp.abs(total), axis=1, keepdims=True), axis=0, keepdims=True)
        power = jnp.minimum(jnp.floor(jnp.log2(224.0 / jnp.maximum(top, 1e-35))), 118.0)
        scale = jnp.exp2(power).astype(jnp.bfloat16).astype(jnp.float32)
        total = jnp.where(column == 0, power, total * scale)
        for h in range(LAGS // LANES):
            rows_ref[h, pitch * k : pitch * k + stations, :] = total[
                :, LANES * h : LANES * (h + 1)
            ]
    for s in range(stations):
        for h in range(LAGS // LANES):
            at = LAGS * s + LANES * h
            out_ref[:, at : at + LANES] = rows_ref[h, pl.ds(s, slices, stride=pitch), :].astype(
                jnp.bfloat16
            )


def correlate(windowed, body, halos, reference_station):
    pols, stations, samples = windowed.shape
    slices = samples // WIN
    pitch = -(-stations // 8) * 8
    params = pltpu.CompilerParams(vmem_limit_bytes=24 << 20)
    part = pl.pallas_call(
        corr_kernel,
        out_shape=jax.ShapeDtypeStruct((pitch * slices, LAGS), jnp.float32),
        in_specs=[VMEM, VMEM],
        out_specs=VMEM,
        scratch_shapes=[
            pltpu.VMEM((8, samples), jnp.float32),
            pltpu.VMEM((pols, LANES, samples), jnp.bfloat16),
        ],
        cost_estimate=pl.CostEstimate(
            flops=2 * pols * stations * samples * LAGS,
            bytes_accessed=2 * pols * stations * samples,
            transcendentals=0,
        ),
        compiler_params=params,
    )(windowed, body)
    return pl.pallas_call(
        functools.partial(finish_kernel, norm_inverse()),
        out_shape=jax.ShapeDtypeStruct((slices, stations * LAGS), jnp.bfloat16),
        in_specs=[SMEM] + [VMEM] * 5,
        out_specs=VMEM,
        scratch_shapes=[pltpu.VMEM((LAGS // LANES, pitch * slices, LANES), jnp.float32)],
        cost_estimate=pl.CostEstimate(
            flops=4 * pols * stations * LAGS * LAGS,
            bytes_accessed=2 * pols * stations * LAGS,
            transcendentals=0,
        ),
        compiler_params=params,
    )(reference_station, windowed, body, *halos, part)


def split_kernel(*refs):
    *block_refs, pieces_ref, scale_ref = refs
    stages = []
    for ref in block_refs:
        block = ref[...].astype(jnp.float32)
        coarse = block.astype(F8).astype(jnp.float32)
        stages.append(jnp.concatenate([coarse, (block - coarse) * 16.0], axis=0))
    pieces_ref[...] = jnp.concatenate(stages, axis=0).astype(F8)
    for d, ref in enumerate(block_refs):
        rows = ref.shape[0]
        power = ref[:, 0:LANES].astype(jnp.float32)[:, 0:1]
        down = jnp.exp2(-power).astype(jnp.bfloat16).astype(jnp.float32)
        down = jnp.broadcast_to(down * (1.0 / math.sqrt(2.0 * STATIONS)), (rows, LANES))
        scale_ref[2 * rows * d : 2 * rows * (d + 1), :] = jnp.concatenate(
            [down, down * (1.0 / 16.0)], axis=0
        )


def split(blocks):
    slices, columns = blocks[0].shape
    rows = 2 * slices * len(blocks)
    return pl.pallas_call(
        split_kernel,
        out_shape=[
            jax.ShapeDtypeStruct((rows, columns), F8),
            jax.ShapeDtypeStruct((rows, LANES), jnp.float32),
        ],
        in_specs=[VMEM] * len(blocks),
        out_specs=[VMEM] * 2,
        cost_estimate=pl.CostEstimate(
            flops=8 * rows * columns, bytes_accessed=2 * rows * columns, transcendentals=0
        ),
        compiler_params=pltpu.CompilerParams(vmem_limit_bytes=16 << 20),
    )(*blocks)


def target_kernel(stations, offset_ref, delay_ref, out_ref, rows_ref, offsets_ref, semaphores):
    rows = rows_ref.shape[0]
    tile, voxels = out_ref.shape[1:]
    first = lax.axis_index("stn") * stations
    start = pl.multiple_of(jnp.minimum(first // 8, (delay_ref.shape[0] - rows) // 8) * 8, 8)
    copies = [
        pltpu.make_async_copy(delay_ref.at[pl.ds(start, rows), :], rows_ref, semaphores.at[0]),
        pltpu.make_async_copy(offset_ref, offsets_ref, semaphores.at[1]),
    ]
    for copy in copies:
        copy.start()
    for copy in copies:
        copy.wait()
    for s in range(stations):
        delays = rows_ref[pl.ds(first - start + s, 1), :]
        target = (HALF - 1 - offsets_ref[first + s]) - delays
        out_ref[s] = jnp.broadcast_to(target, (tile, voxels)).astype(jnp.int8)


def targets(sample_delays, timing_offsets, stations):
    total, voxels = sample_delays.shape
    slack = max(a * stations % 8 for a in range(total // stations))
    rows = min(-(-(slack + stations) // 8) * 8, total)
    return pl.pallas_call(
        functools.partial(target_kernel, stations),
        out_shape=jax.ShapeDtypeStruct((stations, 32, voxels), jnp.int8),
        in_specs=[pl.BlockSpec(memory_space=pltpu.HBM)] * 2,
        out_specs=VMEM,
        scratch_shapes=[
            pltpu.VMEM((rows, voxels), jnp.int32),
            pltpu.SMEM(timing_offsets.shape, jnp.int32),
            pltpu.SemaphoreType.DMA((2,)),
        ],
        cost_estimate=pl.CostEstimate(
            flops=32 * stations * voxels, bytes_accessed=36 * stations * voxels, transcendentals=0
        ),
        compiler_params=pltpu.CompilerParams(vmem_limit_bytes=24 << 20),
    )(timing_offsets, sample_delays)


def image_kernel(swap, parts, start, target_ref, *refs):
    piece_refs, scale_refs = refs[:parts], refs[parts : 2 * parts]
    *out_refs, sums_ref = refs[2 * parts :]
    rows = piece_refs[0].shape[0]
    stations, tile, _ = target_ref.shape
    voxels = sums_ref.shape[1]
    level = (lax.broadcasted_iota(jnp.int32, (LAGS, voxels), 0) - HALF).astype(jnp.int8)
    one = jnp.ones((LAGS, voxels), F8)
    zero = jnp.zeros((LAGS, voxels), F8)
    sums = jnp.zeros((parts * rows, voxels), jnp.float32)
    for s0 in range(0, stations, 2):
        hots = []
        for s in range(s0, min(s0 + 2, stations)):
            target = jnp.concatenate([target_ref[s, :, start : start + voxels]] * (LAGS // tile), axis=0)
            hots.append(jnp.where(level == target, one, zero))
        hot = jnp.concatenate(hots, axis=0) if len(hots) > 1 else hots[0]
        at = LAGS * s0
        pieces = jnp.concatenate([ref[:, at : at + hot.shape[0]] for ref in piece_refs], axis=0)
        sums = sums + jnp.dot(pieces, hot, preferred_element_type=jnp.float32)
    for g in range(parts):
        for r in range(0, rows, 8):
            at = rows * g + r
            sums_ref[at : at + 8, :] = sums[at : at + 8, :] * scale_refs[g][r : r + 8, 0:1]
    mine = lax.axis_index("vox")
    groups = parts * rows // 8
    if swap:
        mine = mine ^ (lax.axis_index("stn") * (groups // 2))
    first = lax.broadcasted_iota(jnp.int32, (8, voxels), 0) < 4
    lower = None
    for j in range(0, groups, 2):
        here, there = mine ^ j, mine ^ (j + 1)
        if swap:
            here, there = [(d & 3) * 4 + d // 4 for d in (here, there)]
        here = sums_ref[pl.ds(pl.multiple_of(8 * here, 8), 8), :]
        there = sums_ref[pl.ds(pl.multiple_of(8 * there, 8), 8), :]
        value = jnp.where(
            first,
            here + pltpu.roll(here, 4, 0),
            there + pltpu.roll(there, 4, 0),
        )
        if not swap or j < groups // 2:
            out_refs[0][4 * j : 4 * j + 8, :] = value
        elif lower is None:
            lower = value
        else:
            at = 4 * (j - groups // 2) - 8
            out_refs[1][at : at + 16, :] = jnp.concatenate([lower, value], axis=0).astype(
                jnp.bfloat16
            )
            lower = None


def image(pieces, scales, target, swap, start, voxels):
    rows, columns = pieces[0].shape
    total = len(pieces) * rows // 2
    if swap:
        out_shape = [
            jax.ShapeDtypeStruct((total // 2, voxels), jnp.float32),
            jax.ShapeDtypeStruct((total // 2, voxels), jnp.bfloat16),
        ]
    else:
        out_shape = [jax.ShapeDtypeStruct((total, voxels), jnp.float32)]
    return pl.pallas_call(
        functools.partial(image_kernel, swap, len(pieces), start),
        out_shape=out_shape,
        in_specs=[VMEM] * (1 + 2 * len(pieces)),
        out_specs=[VMEM] * len(out_shape),
        scratch_shapes=[pltpu.VMEM((2 * total, voxels), jnp.float32)],
        cost_estimate=pl.CostEstimate(
            flops=4 * total * voxels,
            bytes_accessed=total,
            transcendentals=0,
        ),
        compiler_params=pltpu.CompilerParams(vmem_limit_bytes=48 << 20),
    )(target, *pieces, *scales)


def add_kernel(start, kept_ref, came_ref, *refs):
    out_ref, total_ref, semaphore = refs[-3:]
    total_ref[...] = kept_ref[...] + came_ref[...].astype(jnp.float32)
    copy = pltpu.make_async_copy(
        total_ref, out_ref.at[:, pl.ds(start, total_ref.shape[1])], semaphore
    )
    copy.start()
    copy.wait()


def add_part(kept, came, out, start, voxels):
    anywhere = pl.BlockSpec(memory_space=pltpu.HBM)
    before = () if out is None else (out,)
    return pl.pallas_call(
        functools.partial(add_kernel, start),
        out_shape=jax.ShapeDtypeStruct((kept.shape[0], voxels), jnp.float32),
        in_specs=[VMEM, VMEM] + [anywhere] * len(before),
        out_specs=anywhere,
        scratch_shapes=[pltpu.VMEM(kept.shape, jnp.float32), pltpu.SemaphoreType.DMA],
        input_output_aliases={2: 0} if before else {},
        cost_estimate=pl.CostEstimate(
            flops=kept.size, bytes_accessed=4 * kept.size, transcendentals=0
        ),
        compiler_params=pltpu.CompilerParams(vmem_limit_bytes=16 << 20),
    )(kept, came, *before)


def flip(block, axis, mask):
    count = lax.axis_size(axis)
    return lax.ppermute(block, axis, [(i, i ^ mask) for i in range(count)])


def halos_paired(body):
    count = lax.axis_size("vox")
    odd = lax.axis_index("vox") % 2 == 1
    first, last = body[:, :HALF], body[:, body.shape[1] - HALF :]
    steps = [(b, b + 1) for b in range(1, count - 1, 2)]
    steps += [(target, source) for source, target in steps]
    outer = lax.ppermute(jnp.where(odd, last, first), "vox", steps)
    inner = flip(jnp.where(odd, first, last), "vox", 1)
    return jnp.where(odd, inner, outer), jnp.where(odd, outer, inner)


def after(value, *others):
    return lax.optimization_barrier((value, *others))[0]


def gather_paired(block, sample_delays, timing_offsets, stations):
    blocks = {0: block}
    for d in (12, 8, 4, 2):
        blocks[d] = flip(block, "vox", d)
    blocks[1] = flip(block, "vox", 1)
    blocks[6] = flip(blocks[4], "vox", 2)
    target = targets(after(sample_delays, blocks[4]), timing_offsets, stations)
    near, target = lax.optimization_barrier((blocks[8], blocks[4], target, blocks[1]))[::2]
    blocks[10] = flip(near, "vox", 2)
    far = after(blocks[12], near)
    blocks[14] = flip(far, "vox", 2)
    blocks[2], blocks[4], blocks[6], blocks[8], blocks[12] = lax.optimization_barrier(
        (blocks[2], blocks[4], blocks[6], near, far)
    )
    for d in (2, 4, 6):
        blocks[d | 1] = flip(blocks[d], "vox", 1)
    early = split([blocks[d] for d in ORDER[0]])
    gate = lax.optimization_barrier((blocks[8], blocks[12], early, blocks[5]))
    blocks[8], blocks[12], early = gate[:3]
    for d in (8, 12):
        blocks[d | 1] = flip(blocks[d], "vox", 1)
    blocks[11] = flip(blocks[10], "vox", 1)
    blocks[14] = after(blocks[14], blocks[11], blocks[13])
    blocks[15] = flip(blocks[14], "vox", 1)
    middle = split([blocks[d] for d in ORDER[1]])
    return [early, middle] + [split([blocks[d] for d in order]) for order in ORDER[2:]], target


ORDER = ((0, 4, 8, 12), (1, 5, 9, 13), (2, 6, 10, 14), (3, 7, 11, 15))


def shards(voltages, sample_delays, timing_offsets, reference_station):
    stations_here, pols, samples_here = voltages.shape
    slices_here = samples_here // WIN
    count = lax.axis_size("vox")
    station_ref = reference_station[0]
    owner = station_ref // stations_here
    swap = lax.axis_size("stn") == 2 and count == 16

    candidate = lax.dynamic_index_in_dim(voltages, station_ref % stations_here, 0, keepdims=False)
    candidate = lax.optimization_barrier(candidate)
    mine = lax.axis_index("stn") == owner
    if swap:
        body = jnp.where(mine, candidate, flip(candidate, "stn", 1))
        halos = halos_paired(body)
    else:
        body = lax.psum(jnp.where(mine, candidate, 0).astype(candidate.dtype), "stn")
        forward = [(i, i + 1) for i in range(count - 1)]
        backward = [(target, source) for source, target in forward]
        halos = (
            lax.ppermute(body[:, samples_here - HALF :], "vox", forward),
            lax.ppermute(body[:, :HALF], "vox", backward),
        )

    taper = np.tile(taper_weights(), slices_here)
    windowed = (voltages.astype(jnp.float32) * taper).astype(jnp.bfloat16)
    windowed = jnp.transpose(windowed, (1, 0, 2))

    corr = correlate(windowed, body, halos, reference_station)
    if swap:
        pairs, target = gather_paired(corr, sample_delays, timing_offsets, stations_here)
    else:
        target = targets(sample_delays, timing_offsets, stations_here)
        gathered = lax.all_gather(corr, "vox", axis=0, tiled=False)
        place = lax.axis_index("vox")
        every = [
            lax.dynamic_index_in_dim(gathered, place ^ j, 0, keepdims=False) for j in range(count)
        ]
        pairs = [split(every[j : j + 4]) for j in range(0, count, 4)]
    pieces, scales = zip(*pairs, strict=True)
    if not swap:
        (partial,) = image(pieces, scales, target, False, 0, sample_delays.shape[1])
        return lax.psum_scatter(partial, "stn", scatter_dimension=0, tiled=True)
    parts = []
    start = 0
    for share in SHARES:
        voxels = sample_delays.shape[1] * share // sum(SHARES)
        kept, sent = image(pieces, scales, target, True, start, voxels)
        parts.append((start, kept, flip(sent, "stn", 1)))
        start += voxels
    out = None
    for start, kept, came in parts:
        out = add_part(kept, came, out, start, sample_delays.shape[1])
    return out


SHARES = (14, 10, 8)


def solution(mesh):
    return jax.shard_map(
        shards,
        mesh=mesh,
        in_specs=(P("stn", None, "vox"), P(None, "vox"), P(), P()),
        out_specs=P("stn", "vox"),
        check_vma=False,
    )
```

```python
import functools
import math

import jax
import jax.numpy as jnp
import numpy as np
from jax import lax
from jax.experimental import pallas as pl
from jax.experimental.pallas import tpu as pltpu
from jax.sharding import PartitionSpec as P

STATIONS = 56
WIN = 1024
LAGS = 256
HALF = LAGS // 2
LANES = 128
F8 = jnp.float8_e4m3fn
VMEM = pl.BlockSpec(memory_space=pltpu.VMEM)
SMEM = pl.BlockSpec(memory_space=pltpu.SMEM)


def taper_weights():
    position = (np.arange(WIN, dtype=np.float32) + np.float32(0.5)) / np.float32(WIN)
    return (0.5 - 0.5 * np.cos(2.0 * np.pi * position.astype(np.float64))).astype(np.float32)


def norm_inverse():
    taper = taper_weights()
    return float(np.float32(1.0) / np.sqrt(np.sum(taper * taper, dtype=np.float32)))


def lane_gather(table, index):
    return lax.gather(
        table,
        index[..., None],
        lax.GatherDimensionNumbers(
            offset_dims=(),
            collapsed_slice_dims=(1,),
            start_index_map=(1,),
            operand_batching_dims=(0,),
            start_indices_batching_dims=(0,),
        ),
        slice_sizes=(1, 1),
        mode=lax.GatherScatterMode.PROMISE_IN_BOUNDS,
    )


def reverse_block(block):
    mirror = LANES - 1 - lax.broadcasted_iota(jnp.int32, (8, LANES), 1)
    piece = block.astype(jnp.float32)
    return lane_gather(jnp.concatenate([piece] * (8 // piece.shape[0]), axis=0), mirror)


def shifted_copies(pair):
    pair = jnp.broadcast_to(pair, (LANES, 2 * LANES))
    return pltpu.roll(pair, 0, 1, stride=1, stride_axis=0)[:, LANES:].astype(jnp.bfloat16)


def chunk_product(windowed, left, middle, right):
    hankel = jnp.concatenate(
        [jnp.concatenate([middle, right], axis=1), jnp.concatenate([left, middle], axis=1)], axis=0
    )
    return jnp.dot(windowed, hankel, preferred_element_type=jnp.float32)


def corr_kernel(win_ref, ref_ref, out_ref, rev_ref, shift_ref):
    pols, stations, samples = win_ref.shape
    slices = samples // WIN
    pitch = out_ref.shape[0] // slices
    blocks = samples // LANES
    for m in range(blocks):
        at = LANES * (blocks - 1 - m)
        rev_ref[:, at : at + LANES] = reverse_block(ref_ref[:, LANES * m : LANES * (m + 1)])
    for p in range(pols):
        for m in range(1, blocks):
            shift_ref[p, :, LANES * m : LANES * (m + 1)] = shifted_copies(
                rev_ref[p : p + 1, LANES * (m - 1) : LANES * (m + 1)]
            )
    chunks = WIN // LAGS
    for k in range(slices):
        total = jnp.zeros((stations, LAGS), jnp.float32)
        for p in range(pols):
            for a in range(chunks):
                if (k, a) in ((0, 0), (slices - 1, chunks - 1)):
                    continue
                first = WIN * k + LAGS * a
                at = samples - first - LANES
                total = total + chunk_product(
                    win_ref[p, :, first : first + LAGS],
                    shift_ref[p, :, at - LANES : at],
                    shift_ref[p, :, at : at + LANES],
                    shift_ref[p, :, at + LANES : at + 2 * LANES],
                )
        out_ref[pitch * k : pitch * k + stations, :] = total


def finish_kernel(norm, ref_ref, win_ref, body_ref, low_ref, high_ref, part_ref, out_ref, rows_ref):
    pols, stations, samples = win_ref.shape
    slices = samples // WIN
    pitch = part_ref.shape[0] // slices
    early = [reverse_block(body_ref[:, LANES * m : LANES * (m + 1)]) for m in (2, 1, 0)]
    early.append(reverse_block(low_ref[...]))
    ends = samples - LANES
    late = [reverse_block(high_ref[...])]
    late += [
        reverse_block(body_ref[:, ends - LANES * m : ends - LANES * (m - 1)]) for m in (0, 1, 2)
    ]
    extra = []
    for first, row in ((0, early), (samples - LAGS, late)):
        total = jnp.zeros((stations, LAGS), jnp.float32)
        for p in range(pols):
            copies = [
                shifted_copies(jnp.concatenate([row[m][p : p + 1], row[m + 1][p : p + 1]], axis=1))
                for m in range(3)
            ]
            total = total + chunk_product(win_ref[p, :, first : first + LAGS], *copies)
        extra.append(total)
    station = lax.broadcasted_iota(jnp.int32, (stations, LAGS), 0)
    column = lax.broadcasted_iota(jnp.int32, (stations, LAGS), 1)
    mine = ref_ref[0] - lax.axis_index("stn") * stations
    factor = jnp.where((station == mine) | (column == 0), 0.0, norm)
    for k in range(slices):
        total = part_ref[pitch * k : pitch * k + stations, :]
        if k == 0:
            total = total + extra[0]
        if k == slices - 1:
            total = total + extra[1]
        total = total * factor
        top = jnp.max(jnp.max(jnp.abs(total), axis=1, keepdims=True), axis=0, keepdims=True)
        power = jnp.minimum(jnp.floor(jnp.log2(224.0 / jnp.maximum(top, 1e-35))), 118.0)
        scale = jnp.exp2(power).astype(jnp.bfloat16).astype(jnp.float32)
        total = jnp.where(column == 0, power, total * scale)
        for h in range(LAGS // LANES):
            rows_ref[h, pitch * k : pitch * k + stations, :] = total[
                :, LANES * h : LANES * (h + 1)
            ]
    for s in range(stations):
        for h in range(LAGS // LANES):
            at = LAGS * s + LANES * h
            out_ref[:, at : at + LANES] = rows_ref[h, pl.ds(s, slices, stride=pitch), :].astype(
                jnp.bfloat16
            )


def correlate(windowed, body, halos, reference_station):
    pols, stations, samples = windowed.shape
    slices = samples // WIN
    pitch = -(-stations // 8) * 8
    params = pltpu.CompilerParams(vmem_limit_bytes=24 << 20)
    part = pl.pallas_call(
        corr_kernel,
        out_shape=jax.ShapeDtypeStruct((pitch * slices, LAGS), jnp.float32),
        in_specs=[VMEM, VMEM],
        out_specs=VMEM,
        scratch_shapes=[
            pltpu.VMEM((8, samples), jnp.float32),
            pltpu.VMEM((pols, LANES, samples), jnp.bfloat16),
        ],
        cost_estimate=pl.CostEstimate(
            flops=2 * pols * stations * samples * LAGS,
            bytes_accessed=2 * pols * stations * samples,
            transcendentals=0,
        ),
        compiler_params=params,
    )(windowed, body)
    return pl.pallas_call(
        functools.partial(finish_kernel, norm_inverse()),
        out_shape=jax.ShapeDtypeStruct((slices, stations * LAGS), jnp.bfloat16),
        in_specs=[SMEM] + [VMEM] * 5,
        out_specs=VMEM,
        scratch_shapes=[pltpu.VMEM((LAGS // LANES, pitch * slices, LANES), jnp.float32)],
        cost_estimate=pl.CostEstimate(
            flops=4 * pols * stations * LAGS * LAGS,
            bytes_accessed=2 * pols * stations * LAGS,
            transcendentals=0,
        ),
        compiler_params=params,
    )(reference_station, windowed, body, *halos, part)


def split_kernel(*refs):
    *block_refs, pieces_ref, scale_ref = refs
    stages = []
    for ref in block_refs:
        block = ref[...].astype(jnp.float32)
        coarse = block.astype(F8).astype(jnp.float32)
        stages.append(jnp.concatenate([coarse, (block - coarse) * 16.0], axis=0))
    pieces_ref[...] = jnp.concatenate(stages, axis=0).astype(F8)
    for d, ref in enumerate(block_refs):
        rows = ref.shape[0]
        power = ref[:, 0:LANES].astype(jnp.float32)[:, 0:1]
        down = jnp.exp2(-power).astype(jnp.bfloat16).astype(jnp.float32)
        down = jnp.broadcast_to(down * (1.0 / math.sqrt(2.0 * STATIONS)), (rows, LANES))
        scale_ref[2 * rows * d : 2 * rows * (d + 1), :] = jnp.concatenate(
            [down, down * (1.0 / 16.0)], axis=0
        )


def split(blocks):
    slices, columns = blocks[0].shape
    rows = 2 * slices * len(blocks)
    return pl.pallas_call(
        split_kernel,
        out_shape=[
            jax.ShapeDtypeStruct((rows, columns), F8),
            jax.ShapeDtypeStruct((rows, LANES), jnp.float32),
        ],
        in_specs=[VMEM] * len(blocks),
        out_specs=[VMEM] * 2,
        cost_estimate=pl.CostEstimate(
            flops=8 * rows * columns, bytes_accessed=2 * rows * columns, transcendentals=0
        ),
        compiler_params=pltpu.CompilerParams(vmem_limit_bytes=16 << 20),
    )(*blocks)


def target_kernel(stations, offset_ref, delay_ref, out_ref, rows_ref, offsets_ref, semaphores):
    rows = rows_ref.shape[0]
    tile, voxels = out_ref.shape[1:]
    first = lax.axis_index("stn") * stations
    start = pl.multiple_of(jnp.minimum(first // 8, (delay_ref.shape[0] - rows) // 8) * 8, 8)
    copies = [
        pltpu.make_async_copy(delay_ref.at[pl.ds(start, rows), :], rows_ref, semaphores.at[0]),
        pltpu.make_async_copy(offset_ref, offsets_ref, semaphores.at[1]),
    ]
    for copy in copies:
        copy.start()
    for copy in copies:
        copy.wait()
    for s in range(stations):
        delays = rows_ref[pl.ds(first - start + s, 1), :]
        target = (HALF - 1 - offsets_ref[first + s]) - delays
        out_ref[s] = jnp.broadcast_to(target, (tile, voxels)).astype(jnp.int8)


def targets(sample_delays, timing_offsets, stations):
    total, voxels = sample_delays.shape
    slack = max(a * stations % 8 for a in range(total // stations))
    rows = min(-(-(slack + stations) // 8) * 8, total)
    return pl.pallas_call(
        functools.partial(target_kernel, stations),
        out_shape=jax.ShapeDtypeStruct((stations, 32, voxels), jnp.int8),
        in_specs=[pl.BlockSpec(memory_space=pltpu.HBM)] * 2,
        out_specs=VMEM,
        scratch_shapes=[
            pltpu.VMEM((rows, voxels), jnp.int32),
            pltpu.SMEM(timing_offsets.shape, jnp.int32),
            pltpu.SemaphoreType.DMA((2,)),
        ],
        cost_estimate=pl.CostEstimate(
            flops=32 * stations * voxels, bytes_accessed=36 * stations * voxels, transcendentals=0
        ),
        compiler_params=pltpu.CompilerParams(vmem_limit_bytes=24 << 20),
    )(timing_offsets, sample_delays)


def image_kernel(swap, parts, start, target_ref, *refs):
    piece_refs, scale_refs = refs[:parts], refs[parts : 2 * parts]
    *out_refs, sums_ref = refs[2 * parts :]
    rows = piece_refs[0].shape[0]
    stations, tile, _ = target_ref.shape
    voxels = sums_ref.shape[1]
    level = (lax.broadcasted_iota(jnp.int32, (LAGS, voxels), 0) - HALF).astype(jnp.int8)
    one = jnp.ones((LAGS, voxels), F8)
    zero = jnp.zeros((LAGS, voxels), F8)
    sums = jnp.zeros((parts * rows, voxels), jnp.float32)
    for s0 in range(0, stations, 2):
        hots = []
        for s in range(s0, min(s0 + 2, stations)):
            target = jnp.concatenate([target_ref[s, :, start : start + voxels]] * (LAGS // tile), axis=0)
            hots.append(jnp.where(level == target, one, zero))
        hot = jnp.concatenate(hots, axis=0) if len(hots) > 1 else hots[0]
        at = LAGS * s0
        pieces = jnp.concatenate([ref[:, at : at + hot.shape[0]] for ref in piece_refs], axis=0)
        sums = sums + jnp.dot(pieces, hot, preferred_element_type=jnp.float32)
    for g in range(parts):
        for r in range(0, rows, 8):
            at = rows * g + r
            sums_ref[at : at + 8, :] = sums[at : at + 8, :] * scale_refs[g][r : r + 8, 0:1]
    mine = lax.axis_index("vox")
    groups = parts * rows // 8
    if swap:
        mine = mine ^ (lax.axis_index("stn") * (groups // 2))
    first = lax.broadcasted_iota(jnp.int32, (8, voxels), 0) < 4
    lower = None
    for j in range(0, groups, 2):
        here, there = mine ^ j, mine ^ (j + 1)
        if swap:
            here, there = [(d & 3) * 4 + d // 4 for d in (here, there)]
        here = sums_ref[pl.ds(pl.multiple_of(8 * here, 8), 8), :]
        there = sums_ref[pl.ds(pl.multiple_of(8 * there, 8), 8), :]
        value = jnp.where(
            first,
            here + pltpu.roll(here, 4, 0),
            there + pltpu.roll(there, 4, 0),
        )
        if not swap or j < groups // 2:
            out_refs[0][4 * j : 4 * j + 8, :] = value
        elif lower is None:
            lower = value
        else:
            at = 4 * (j - groups // 2) - 8
            out_refs[1][at : at + 16, :] = jnp.concatenate([lower, value], axis=0).astype(
                jnp.bfloat16
            )
            lower = None


def image(pieces, scales, target, swap, start, voxels):
    rows, columns = pieces[0].shape
    total = len(pieces) * rows // 2
    if swap:
        out_shape = [
            jax.ShapeDtypeStruct((total // 2, voxels), jnp.float32),
            jax.ShapeDtypeStruct((total // 2, voxels), jnp.bfloat16),
        ]
    else:
        out_shape = [jax.ShapeDtypeStruct((total, voxels), jnp.float32)]
    return pl.pallas_call(
        functools.partial(image_kernel, swap, len(pieces), start),
        out_shape=out_shape,
        in_specs=[VMEM] * (1 + 2 * len(pieces)),
        out_specs=[VMEM] * len(out_shape),
        scratch_shapes=[pltpu.VMEM((2 * total, voxels), jnp.float32)],
        cost_estimate=pl.CostEstimate(
            flops=4 * total * voxels,
            bytes_accessed=total,
            transcendentals=0,
        ),
        compiler_params=pltpu.CompilerParams(vmem_limit_bytes=48 << 20),
    )(target, *pieces, *scales)


def add_kernel(start, kept_ref, came_ref, *refs):
    out_ref, total_ref, semaphore = refs[-3:]
    total_ref[...] = kept_ref[...] + came_ref[...].astype(jnp.float32)
    copy = pltpu.make_async_copy(
        total_ref, out_ref.at[:, pl.ds(start, total_ref.shape[1])], semaphore
    )
    copy.start()
    copy.wait()


def add_part(kept, came, out, start, voxels):
    anywhere = pl.BlockSpec(memory_space=pltpu.HBM)
    before = () if out is None else (out,)
    return pl.pallas_call(
        functools.partial(add_kernel, start),
        out_shape=jax.ShapeDtypeStruct((kept.shape[0], voxels), jnp.float32),
        in_specs=[VMEM, VMEM] + [anywhere] * len(before),
        out_specs=anywhere,
        scratch_shapes=[pltpu.VMEM(kept.shape, jnp.float32), pltpu.SemaphoreType.DMA],
        input_output_aliases={2: 0} if before else {},
        cost_estimate=pl.CostEstimate(
            flops=kept.size, bytes_accessed=4 * kept.size, transcendentals=0
        ),
        compiler_params=pltpu.CompilerParams(vmem_limit_bytes=16 << 20),
    )(kept, came, *before)


def flip(block, axis, mask):
    count = lax.axis_size(axis)
    return lax.ppermute(block, axis, [(i, i ^ mask) for i in range(count)])


def halos_paired(body):
    count = lax.axis_size("vox")
    odd = lax.axis_index("vox") % 2 == 1
    first, last = body[:, :HALF], body[:, body.shape[1] - HALF :]
    steps = [(b, b + 1) for b in range(1, count - 1, 2)]
    steps += [(target, source) for source, target in steps]
    outer = lax.ppermute(jnp.where(odd, last, first), "vox", steps)
    inner = flip(jnp.where(odd, first, last), "vox", 1)
    return jnp.where(odd, inner, outer), jnp.where(odd, outer, inner)


def after(value, *others):
    return lax.optimization_barrier((value, *others))[0]


def gather_paired(block, sample_delays, timing_offsets, stations):
    blocks = {0: block}
    for d in (12, 8, 4, 2):
        blocks[d] = flip(block, "vox", d)
    blocks[1] = flip(block, "vox", 1)
    blocks[6] = flip(blocks[4], "vox", 2)
    target = targets(after(sample_delays, blocks[4]), timing_offsets, stations)
    near, target = lax.optimization_barrier((blocks[8], blocks[4], target, blocks[1]))[::2]
    blocks[10] = flip(near, "vox", 2)
    far = after(blocks[12], near)
    blocks[14] = flip(far, "vox", 2)
    blocks[2], blocks[4], blocks[6], blocks[8], blocks[12] = lax.optimization_barrier(
        (blocks[2], blocks[4], blocks[6], near, far)
    )
    for d in (2, 4, 6):
        blocks[d | 1] = flip(blocks[d], "vox", 1)
    early = split([blocks[d] for d in ORDER[0]])
    gate = lax.optimization_barrier((blocks[8], blocks[12], early))
    blocks[8], blocks[12], early = gate[:3]
    for d in (8, 12):
        blocks[d | 1] = flip(blocks[d], "vox", 1)
    blocks[10] = after(blocks[10], blocks[5], blocks[3])
    blocks[11] = flip(blocks[10], "vox", 1)
    blocks[14] = after(blocks[14], blocks[13])
    blocks[15] = flip(blocks[14], "vox", 1)
    middle = split([blocks[d] for d in ORDER[1]])
    return [early, middle] + [split([blocks[d] for d in order]) for order in ORDER[2:]], target


ORDER = ((0, 4, 8, 12), (1, 5, 9, 13), (2, 6, 10, 14), (3, 7, 11, 15))


def shards(voltages, sample_delays, timing_offsets, reference_station):
    stations_here, pols, samples_here = voltages.shape
    slices_here = samples_here // WIN
    count = lax.axis_size("vox")
    station_ref = reference_station[0]
    owner = station_ref // stations_here
    swap = lax.axis_size("stn") == 2 and count == 16

    candidate = lax.dynamic_index_in_dim(voltages, station_ref % stations_here, 0, keepdims=False)
    candidate = lax.optimization_barrier(candidate)
    mine = lax.axis_index("stn") == owner
    if swap:
        body = jnp.where(mine, candidate, flip(candidate, "stn", 1))
        halos = halos_paired(body)
    else:
        body = lax.psum(jnp.where(mine, candidate, 0).astype(candidate.dtype), "stn")
        forward = [(i, i + 1) for i in range(count - 1)]
        backward = [(target, source) for source, target in forward]
        halos = (
            lax.ppermute(body[:, samples_here - HALF :], "vox", forward),
            lax.ppermute(body[:, :HALF], "vox", backward),
        )

    taper = np.tile(taper_weights(), slices_here)
    windowed = (voltages.astype(jnp.float32) * taper).astype(jnp.bfloat16)
    windowed = jnp.transpose(windowed, (1, 0, 2))

    corr = correlate(windowed, body, halos, reference_station)
    if swap:
        pairs, target = gather_paired(corr, sample_delays, timing_offsets, stations_here)
    else:
        target = targets(sample_delays, timing_offsets, stations_here)
        gathered = lax.all_gather(corr, "vox", axis=0, tiled=False)
        place = lax.axis_index("vox")
        every = [
            lax.dynamic_index_in_dim(gathered, place ^ j, 0, keepdims=False) for j in range(count)
        ]
        pairs = [split(every[j : j + 4]) for j in range(0, count, 4)]
    pieces, scales = zip(*pairs, strict=True)
    if not swap:
        (partial,) = image(pieces, scales, target, False, 0, sample_delays.shape[1])
        return lax.psum_scatter(partial, "stn", scatter_dimension=0, tiled=True)
    parts = []
    start = 0
    for share in SHARES:
        voxels = sample_delays.shape[1] * share // sum(SHARES)
        kept, sent = image(pieces, scales, target, True, start, voxels)
        parts.append((start, kept, flip(sent, "stn", 1)))
        start += voxels
    out = None
    for start, kept, came in parts:
        out = add_part(kept, came, out, start, sample_delays.shape[1])
    return out


SHARES = (14, 10, 8)


def solution(mesh):
    return jax.shard_map(
        shards,
        mesh=mesh,
        in_specs=(P("stn", None, "vox"), P(None, "vox"), P(), P()),
        out_specs=P("stn", "vox"),
        check_vma=False,
    )
```

```python
import functools
import math

import jax
import jax.numpy as jnp
import numpy as np
from jax import lax
from jax.experimental import pallas as pl
from jax.experimental.pallas import tpu as pltpu
from jax.sharding import PartitionSpec as P

STATIONS = 56
WIN = 1024
LAGS = 256
HALF = LAGS // 2
LANES = 128
F8 = jnp.float8_e4m3fn
VMEM = pl.BlockSpec(memory_space=pltpu.VMEM)
SMEM = pl.BlockSpec(memory_space=pltpu.SMEM)


def taper_weights():
    position = (np.arange(WIN, dtype=np.float32) + np.float32(0.5)) / np.float32(WIN)
    return (0.5 - 0.5 * np.cos(2.0 * np.pi * position.astype(np.float64))).astype(np.float32)


def norm_inverse():
    taper = taper_weights()
    return float(np.float32(1.0) / np.sqrt(np.sum(taper * taper, dtype=np.float32)))


def lane_gather(table, index):
    return lax.gather(
        table,
        index[..., None],
        lax.GatherDimensionNumbers(
            offset_dims=(),
            collapsed_slice_dims=(1,),
            start_index_map=(1,),
            operand_batching_dims=(0,),
            start_indices_batching_dims=(0,),
        ),
        slice_sizes=(1, 1),
        mode=lax.GatherScatterMode.PROMISE_IN_BOUNDS,
    )


def reverse_block(block):
    mirror = LANES - 1 - lax.broadcasted_iota(jnp.int32, (8, LANES), 1)
    piece = block.astype(jnp.float32)
    return lane_gather(jnp.concatenate([piece] * (8 // piece.shape[0]), axis=0), mirror)


def shifted_copies(pair):
    pair = jnp.broadcast_to(pair, (LANES, 2 * LANES))
    return pltpu.roll(pair, 0, 1, stride=1, stride_axis=0)[:, LANES:].astype(jnp.bfloat16)


def chunk_product(windowed, left, middle, right):
    hankel = jnp.concatenate(
        [jnp.concatenate([middle, right], axis=1), jnp.concatenate([left, middle], axis=1)], axis=0
    )
    return jnp.dot(windowed, hankel, preferred_element_type=jnp.float32)


def corr_kernel(win_ref, ref_ref, out_ref, rev_ref, shift_ref):
    pols, stations, samples = win_ref.shape
    slices = samples // WIN
    pitch = out_ref.shape[0] // slices
    blocks = samples // LANES
    for m in range(blocks):
        at = LANES * (blocks - 1 - m)
        rev_ref[:, at : at + LANES] = reverse_block(ref_ref[:, LANES * m : LANES * (m + 1)])
    for p in range(pols):
        for m in range(1, blocks):
            shift_ref[p, :, LANES * m : LANES * (m + 1)] = shifted_copies(
                rev_ref[p : p + 1, LANES * (m - 1) : LANES * (m + 1)]
            )
    chunks = WIN // LAGS
    for k in range(slices):
        total = jnp.zeros((stations, LAGS), jnp.float32)
        for p in range(pols):
            for a in range(chunks):
                if (k, a) in ((0, 0), (slices - 1, chunks - 1)):
                    continue
                first = WIN * k + LAGS * a
                at = samples - first - LANES
                total = total + chunk_product(
                    win_ref[p, :, first : first + LAGS],
                    shift_ref[p, :, at - LANES : at],
                    shift_ref[p, :, at : at + LANES],
                    shift_ref[p, :, at + LANES : at + 2 * LANES],
                )
        out_ref[pitch * k : pitch * k + stations, :] = total


def finish_kernel(norm, ref_ref, win_ref, body_ref, low_ref, high_ref, part_ref, out_ref, rows_ref):
    pols, stations, samples = win_ref.shape
    slices = samples // WIN
    pitch = part_ref.shape[0] // slices
    early = [reverse_block(body_ref[:, LANES * m : LANES * (m + 1)]) for m in (2, 1, 0)]
    early.append(reverse_block(low_ref[...]))
    ends = samples - LANES
    late = [reverse_block(high_ref[...])]
    late += [
        reverse_block(body_ref[:, ends - LANES * m : ends - LANES * (m - 1)]) for m in (0, 1, 2)
    ]
    extra = []
    for first, row in ((0, early), (samples - LAGS, late)):
        total = jnp.zeros((stations, LAGS), jnp.float32)
        for p in range(pols):
            copies = [
                shifted_copies(jnp.concatenate([row[m][p : p + 1], row[m + 1][p : p + 1]], axis=1))
                for m in range(3)
            ]
            total = total + chunk_product(win_ref[p, :, first : first + LAGS], *copies)
        extra.append(total)
    station = lax.broadcasted_iota(jnp.int32, (stations, LAGS), 0)
    column = lax.broadcasted_iota(jnp.int32, (stations, LAGS), 1)
    mine = ref_ref[0] - lax.axis_index("stn") * stations
    factor = jnp.where((station == mine) | (column == 0), 0.0, norm)
    for k in range(slices):
        total = part_ref[pitch * k : pitch * k + stations, :]
        if k == 0:
            total = total + extra[0]
        if k == slices - 1:
            total = total + extra[1]
        total = total * factor
        top = jnp.max(jnp.max(jnp.abs(total), axis=1, keepdims=True), axis=0, keepdims=True)
        power = jnp.minimum(jnp.floor(jnp.log2(224.0 / jnp.maximum(top, 1e-35))), 118.0)
        scale = jnp.exp2(power).astype(jnp.bfloat16).astype(jnp.float32)
        total = jnp.where(column == 0, power, total * scale)
        for h in range(LAGS // LANES):
            rows_ref[h, pitch * k : pitch * k + stations, :] = total[
                :, LANES * h : LANES * (h + 1)
            ]
    for s in range(stations):
        for h in range(LAGS // LANES):
            at = LAGS * s + LANES * h
            out_ref[:, at : at + LANES] = rows_ref[h, pl.ds(s, slices, stride=pitch), :].astype(
                jnp.bfloat16
            )


def correlate(windowed, body, halos, reference_station):
    pols, stations, samples = windowed.shape
    slices = samples // WIN
    pitch = -(-stations // 8) * 8
    params = pltpu.CompilerParams(vmem_limit_bytes=24 << 20)
    part = pl.pallas_call(
        corr_kernel,
        out_shape=jax.ShapeDtypeStruct((pitch * slices, LAGS), jnp.float32),
        in_specs=[VMEM, VMEM],
        out_specs=VMEM,
        scratch_shapes=[
            pltpu.VMEM((8, samples), jnp.float32),
            pltpu.VMEM((pols, LANES, samples), jnp.bfloat16),
        ],
        cost_estimate=pl.CostEstimate(
            flops=2 * pols * stations * samples * LAGS,
            bytes_accessed=2 * pols * stations * samples,
            transcendentals=0,
        ),
        compiler_params=params,
    )(windowed, body)
    return pl.pallas_call(
        functools.partial(finish_kernel, norm_inverse()),
        out_shape=jax.ShapeDtypeStruct((slices, stations * LAGS), jnp.bfloat16),
        in_specs=[SMEM] + [VMEM] * 5,
        out_specs=VMEM,
        scratch_shapes=[pltpu.VMEM((LAGS // LANES, pitch * slices, LANES), jnp.float32)],
        cost_estimate=pl.CostEstimate(
            flops=4 * pols * stations * LAGS * LAGS,
            bytes_accessed=2 * pols * stations * LAGS,
            transcendentals=0,
        ),
        compiler_params=params,
    )(reference_station, windowed, body, *halos, part)


def split_kernel(*refs):
    *block_refs, pieces_ref, scale_ref = refs
    stages = []
    for ref in block_refs:
        block = ref[...].astype(jnp.float32)
        coarse = block.astype(F8).astype(jnp.float32)
        stages.append(jnp.concatenate([coarse, (block - coarse) * 16.0], axis=0))
    pieces_ref[...] = jnp.concatenate(stages, axis=0).astype(F8)
    for d, ref in enumerate(block_refs):
        rows = ref.shape[0]
        power = ref[:, 0:LANES].astype(jnp.float32)[:, 0:1]
        down = jnp.exp2(-power).astype(jnp.bfloat16).astype(jnp.float32)
        down = jnp.broadcast_to(down * (1.0 / math.sqrt(2.0 * STATIONS)), (rows, LANES))
        scale_ref[2 * rows * d : 2 * rows * (d + 1), :] = jnp.concatenate(
            [down, down * (1.0 / 16.0)], axis=0
        )


def split(blocks):
    slices, columns = blocks[0].shape
    rows = 2 * slices * len(blocks)
    return pl.pallas_call(
        split_kernel,
        out_shape=[
            jax.ShapeDtypeStruct((rows, columns), F8),
            jax.ShapeDtypeStruct((rows, LANES), jnp.float32),
        ],
        in_specs=[VMEM] * len(blocks),
        out_specs=[VMEM] * 2,
        cost_estimate=pl.CostEstimate(
            flops=8 * rows * columns, bytes_accessed=2 * rows * columns, transcendentals=0
        ),
        compiler_params=pltpu.CompilerParams(vmem_limit_bytes=16 << 20),
    )(*blocks)


def target_kernel(stations, offset_ref, delay_ref, out_ref, rows_ref, offsets_ref, semaphores):
    rows = rows_ref.shape[0]
    tile, voxels = out_ref.shape[1:]
    first = lax.axis_index("stn") * stations
    start = pl.multiple_of(jnp.minimum(first // 8, (delay_ref.shape[0] - rows) // 8) * 8, 8)
    copies = [
        pltpu.make_async_copy(delay_ref.at[pl.ds(start, rows), :], rows_ref, semaphores.at[0]),
        pltpu.make_async_copy(offset_ref, offsets_ref, semaphores.at[1]),
    ]
    for copy in copies:
        copy.start()
    for copy in copies:
        copy.wait()
    for s in range(stations):
        delays = rows_ref[pl.ds(first - start + s, 1), :]
        target = (HALF - 1 - offsets_ref[first + s]) - delays
        out_ref[s] = jnp.broadcast_to(target, (tile, voxels)).astype(jnp.int8)


def targets(sample_delays, timing_offsets, stations):
    total, voxels = sample_delays.shape
    slack = max(a * stations % 8 for a in range(total // stations))
    rows = min(-(-(slack + stations) // 8) * 8, total)
    return pl.pallas_call(
        functools.partial(target_kernel, stations),
        out_shape=jax.ShapeDtypeStruct((stations, 32, voxels), jnp.int8),
        in_specs=[pl.BlockSpec(memory_space=pltpu.HBM)] * 2,
        out_specs=VMEM,
        scratch_shapes=[
            pltpu.VMEM((rows, voxels), jnp.int32),
            pltpu.SMEM(timing_offsets.shape, jnp.int32),
            pltpu.SemaphoreType.DMA((2,)),
        ],
        cost_estimate=pl.CostEstimate(
            flops=32 * stations * voxels, bytes_accessed=36 * stations * voxels, transcendentals=0
        ),
        compiler_params=pltpu.CompilerParams(vmem_limit_bytes=24 << 20),
    )(timing_offsets, sample_delays)


def image_kernel(swap, parts, start, target_ref, *refs):
    piece_refs, scale_refs = refs[:parts], refs[parts : 2 * parts]
    *out_refs, sums_ref = refs[2 * parts :]
    rows = piece_refs[0].shape[0]
    stations, tile, _ = target_ref.shape
    voxels = sums_ref.shape[1]
    level = (lax.broadcasted_iota(jnp.int32, (LAGS, voxels), 0) - HALF).astype(jnp.int8)
    one = jnp.ones((LAGS, voxels), F8)
    zero = jnp.zeros((LAGS, voxels), F8)
    sums = jnp.zeros((parts * rows, voxels), jnp.float32)
    for s0 in range(0, stations, 2):
        hots = []
        for s in range(s0, min(s0 + 2, stations)):
            target = jnp.concatenate([target_ref[s, :, start : start + voxels]] * (LAGS // tile), axis=0)
            hots.append(jnp.where(level == target, one, zero))
        hot = jnp.concatenate(hots, axis=0) if len(hots) > 1 else hots[0]
        at = LAGS * s0
        pieces = jnp.concatenate([ref[:, at : at + hot.shape[0]] for ref in piece_refs], axis=0)
        sums = sums + jnp.dot(pieces, hot, preferred_element_type=jnp.float32)
    for g in range(parts):
        for r in range(0, rows, 8):
            at = rows * g + r
            sums_ref[at : at + 8, :] = sums[at : at + 8, :] * scale_refs[g][r : r + 8, 0:1]
    mine = lax.axis_index("vox")
    groups = parts * rows // 8
    if swap:
        mine = mine ^ (lax.axis_index("stn") * (groups // 2))
    first = lax.broadcasted_iota(jnp.int32, (8, voxels), 0) < 4
    lower = None
    for j in range(0, groups, 2):
        here, there = mine ^ j, mine ^ (j + 1)
        if swap:
            here, there = [(d & 3) * 4 + d // 4 for d in (here, there)]
        here = sums_ref[pl.ds(pl.multiple_of(8 * here, 8), 8), :]
        there = sums_ref[pl.ds(pl.multiple_of(8 * there, 8), 8), :]
        value = jnp.where(
            first,
            here + pltpu.roll(here, 4, 0),
            there + pltpu.roll(there, 4, 0),
        )
        if not swap or j < groups // 2:
            out_refs[0][4 * j : 4 * j + 8, :] = value
        elif lower is None:
            lower = value
        else:
            at = 4 * (j - groups // 2) - 8
            out_refs[1][at : at + 16, :] = jnp.concatenate([lower, value], axis=0).astype(
                jnp.bfloat16
            )
            lower = None


def image(pieces, scales, target, swap, start, voxels):
    rows, columns = pieces[0].shape
    total = len(pieces) * rows // 2
    if swap:
        out_shape = [
            jax.ShapeDtypeStruct((total // 2, voxels), jnp.float32),
            jax.ShapeDtypeStruct((total // 2, voxels), jnp.bfloat16),
        ]
    else:
        out_shape = [jax.ShapeDtypeStruct((total, voxels), jnp.float32)]
    return pl.pallas_call(
        functools.partial(image_kernel, swap, len(pieces), start),
        out_shape=out_shape,
        in_specs=[VMEM] * (1 + 2 * len(pieces)),
        out_specs=[VMEM] * len(out_shape),
        scratch_shapes=[pltpu.VMEM((2 * total, voxels), jnp.float32)],
        cost_estimate=pl.CostEstimate(
            flops=4 * total * voxels,
            bytes_accessed=total,
            transcendentals=0,
        ),
        compiler_params=pltpu.CompilerParams(vmem_limit_bytes=48 << 20),
    )(target, *pieces, *scales)


def add_kernel(start, kept_ref, came_ref, *refs):
    out_ref, total_ref, semaphore = refs[-3:]
    total_ref[...] = kept_ref[...] + came_ref[...].astype(jnp.float32)
    copy = pltpu.make_async_copy(
        total_ref, out_ref.at[:, pl.ds(start, total_ref.shape[1])], semaphore
    )
    copy.start()
    copy.wait()


def add_part(kept, came, out, start, voxels):
    anywhere = pl.BlockSpec(memory_space=pltpu.HBM)
    before = () if out is None else (out,)
    return pl.pallas_call(
        functools.partial(add_kernel, start),
        out_shape=jax.ShapeDtypeStruct((kept.shape[0], voxels), jnp.float32),
        in_specs=[VMEM, VMEM] + [anywhere] * len(before),
        out_specs=anywhere,
        scratch_shapes=[pltpu.VMEM(kept.shape, jnp.float32), pltpu.SemaphoreType.DMA],
        input_output_aliases={2: 0} if before else {},
        cost_estimate=pl.CostEstimate(
            flops=kept.size, bytes_accessed=4 * kept.size, transcendentals=0
        ),
        compiler_params=pltpu.CompilerParams(vmem_limit_bytes=16 << 20),
    )(kept, came, *before)


def flip(block, axis, mask):
    count = lax.axis_size(axis)
    return lax.ppermute(block, axis, [(i, i ^ mask) for i in range(count)])


def halos_paired(body):
    count = lax.axis_size("vox")
    odd = lax.axis_index("vox") % 2 == 1
    first, last = body[:, :HALF], body[:, body.shape[1] - HALF :]
    steps = [(b, b + 1) for b in range(1, count - 1, 2)]
    steps += [(target, source) for source, target in steps]
    outer = lax.ppermute(jnp.where(odd, last, first), "vox", steps)
    inner = flip(jnp.where(odd, first, last), "vox", 1)
    return jnp.where(odd, inner, outer), jnp.where(odd, outer, inner)


def after(value, *others):
    return lax.optimization_barrier((value, *others))[0]


def gather_paired(block, sample_delays, timing_offsets, stations):
    blocks = {0: block}
    for d in (12, 8, 4, 2):
        blocks[d] = flip(block, "vox", d)
    blocks[1] = flip(block, "vox", 1)
    blocks[6] = flip(blocks[4], "vox", 2)
    target = targets(after(sample_delays, blocks[4]), timing_offsets, stations)
    near, target = lax.optimization_barrier((blocks[8], blocks[4], target, blocks[1]))[::2]
    blocks[10] = flip(near, "vox", 2)
    far = after(blocks[12], near)
    blocks[14] = flip(far, "vox", 2)
    blocks[2], blocks[4], blocks[6], blocks[8], blocks[12] = lax.optimization_barrier(
        (blocks[2], blocks[4], blocks[6], near, far)
    )
    for d in (2, 4, 6):
        blocks[d | 1] = flip(blocks[d], "vox", 1)
    early = split([blocks[d] for d in ORDER[0]])
    gate = lax.optimization_barrier((blocks[8], blocks[12], early))
    blocks[8], blocks[12], early = gate[:3]
    for d in (8, 12):
        blocks[d | 1] = flip(blocks[d], "vox", 1)
    blocks[10] = after(blocks[10], blocks[7])
    blocks[11] = flip(blocks[10], "vox", 1)
    blocks[14] = after(blocks[14], blocks[13])
    blocks[15] = flip(blocks[14], "vox", 1)
    middle = split([blocks[d] for d in ORDER[1]])
    return [early, middle] + [split([blocks[d] for d in order]) for order in ORDER[2:]], target


ORDER = ((0, 4, 8, 12), (1, 5, 9, 13), (2, 6, 10, 14), (3, 7, 11, 15))


def shards(voltages, sample_delays, timing_offsets, reference_station):
    stations_here, pols, samples_here = voltages.shape
    slices_here = samples_here // WIN
    count = lax.axis_size("vox")
    station_ref = reference_station[0]
    owner = station_ref // stations_here
    swap = lax.axis_size("stn") == 2 and count == 16

    candidate = lax.dynamic_index_in_dim(voltages, station_ref % stations_here, 0, keepdims=False)
    candidate = lax.optimization_barrier(candidate)
    mine = lax.axis_index("stn") == owner
    if swap:
        body = jnp.where(mine, candidate, flip(candidate, "stn", 1))
        halos = halos_paired(body)
    else:
        body = lax.psum(jnp.where(mine, candidate, 0).astype(candidate.dtype), "stn")
        forward = [(i, i + 1) for i in range(count - 1)]
        backward = [(target, source) for source, target in forward]
        halos = (
            lax.ppermute(body[:, samples_here - HALF :], "vox", forward),
            lax.ppermute(body[:, :HALF], "vox", backward),
        )

    taper = np.tile(taper_weights(), slices_here)
    windowed = (voltages.astype(jnp.float32) * taper).astype(jnp.bfloat16)
    windowed = jnp.transpose(windowed, (1, 0, 2))

    corr = correlate(windowed, body, halos, reference_station)
    if swap:
        pairs, target = gather_paired(corr, sample_delays, timing_offsets, stations_here)
    else:
        target = targets(sample_delays, timing_offsets, stations_here)
        gathered = lax.all_gather(corr, "vox", axis=0, tiled=False)
        place = lax.axis_index("vox")
        every = [
            lax.dynamic_index_in_dim(gathered, place ^ j, 0, keepdims=False) for j in range(count)
        ]
        pairs = [split(every[j : j + 4]) for j in range(0, count, 4)]
    pieces, scales = zip(*pairs, strict=True)
    if not swap:
        (partial,) = image(pieces, scales, target, False, 0, sample_delays.shape[1])
        return lax.psum_scatter(partial, "stn", scatter_dimension=0, tiled=True)
    parts = []
    start = 0
    for share in SHARES:
        voxels = sample_delays.shape[1] * share // sum(SHARES)
        kept, sent = image(pieces, scales, target, True, start, voxels)
        parts.append((start, kept, flip(sent, "stn", 1)))
        start += voxels
    out = None
    for start, kept, came in parts:
        out = add_part(kept, came, out, start, sample_delays.shape[1])
    return out


SHARES = (14, 10, 8)


def solution(mesh):
    return jax.shard_map(
        shards,
        mesh=mesh,
        in_specs=(P("stn", None, "vox"), P(None, "vox"), P(), P()),
        out_specs=P("stn", "vox"),
        check_vma=False,
    )
```
